32 devices in a mesh: dp: 2 (over y), space: 16 (over z, x, core).
Axes of the slice: x: 2, y: 2, z: 4, core: 2. Of those that a mesh axis runs over, the one named last changes fastest.
Arguments:
- fields: bfloat16 [2, 32, 32, 64, 256], P('dp', None, 'space'), may hold values from -6 to 6
- cotangent: bfloat16 [2, 32, 32, 64, 256], P('dp', None, 'space'), may hold values from -6 to 6
- mix_weight: bfloat16 [32, 32], replicated, may hold values from -1 to 1
- spectral_weight: bfloat16 [32, 2, 32, 32, 256], P('space'), may hold values from -0.75 to 0.75
Outputs:
- layer_out: bfloat16 [2, 32, 32, 64, 256], P('dp', None, 'space')
- field_grad: bfloat16 [2, 32, 32, 64, 256], P('dp', None, 'space')
- weight_grad: bfloat16 [32, 2, 32, 32, 256], P('space')
The draws below stay inside these ranges and needn't reach their ends.
All inputs are finite; a program needn't handle non-finite values.
Results may differ from the reference program's by a relative error of at most 0.018.
Values may be sent and summed in bfloat16 or wider, within the bound.
A program may use at most 128 MiB of HBM per device.

```python
import math
from functools import partial
import jax
import jax.numpy as jnp
from jax import lax

C = 32
NY = 64
NZ = 64
NT = 4
MX = 16
MY = 16
MZ = 16
MT = 2
S_DEV = 1
NX = 32
BATCH = 2
N_DP = 2


def block_levels(key, shape, pieces, least, largest):
    loudness = 1.0
    for dim, parts in pieces:
        heights = jax.random.uniform(jax.random.fold_in(jax.random.fold_in(key, 6), dim), (parts,), jnp.float32, least / len(pieces), largest / len(pieces))
        loudness = loudness * jnp.repeat(jnp.exp(heights), shape[dim] // parts).reshape((-1,) + (1,) * (len(shape) - 1 - dim))
    return loudness


def centred(rng, dims, spread, limit, shards=(), kind=jnp.bfloat16):
    factor_of = block_levels(rng, dims, shards, -0.22, 0.18) if shards else 1.0
    drawn = jax.random.normal(rng, dims, jnp.float32) * spread * factor_of
    return jnp.minimum(jnp.maximum(drawn, -limit), limit).astype(kind)


def setup_inputs(seed: int = 0) -> dict:
    keys = jax.random.split(jax.random.key(seed), 5)
    fields = centred(keys[0], (BATCH, C, NX, NY, NZ * NT), 1.0, 6.0, ((0, 2), (2, 16)))
    cotangent = centred(keys[1], (BATCH, C, NX, NY, NZ * NT), 1.0, 6.0, ((0, 2), (2, 16)))
    mix_weight = centred(keys[2], (C, C), C ** -0.5, 1.0)
    spectral_weight = centred(keys[3], (MZ * MT, 2, C, C, MX * MY), (2 * C) ** -0.5, 0.75, ((0, 16),))
    return dict(fields=fields, cotangent=cotangent, mix_weight=mix_weight, spectral_weight=spectral_weight)


def line_table(length, mode_count, orient, factor):
    position = jnp.arange(length, dtype=jnp.int32)
    frequency = jnp.arange(mode_count, dtype=jnp.int32) - mode_count // 2
    rotations = position[:, None] * frequency[None, :] % length
    phases = 2.0 * math.pi / length * rotations.astype(jnp.float32)
    return (jnp.cos(phases) * factor, orient * jnp.sin(phases) * factor)

def plane_phases(depth, steps, depth_modes, step_modes):
    cells = jnp.arange(depth * steps, dtype=jnp.int32)
    wavenumbers = jnp.arange(depth_modes * step_modes, dtype=jnp.int32)
    depth_turn = (cells // steps)[:, None] * (wavenumbers // step_modes - depth_modes // 2)[None, :] % depth
    step_turn = (cells % steps)[:, None] * (wavenumbers % step_modes)[None, :] % steps
    return 2.0 * math.pi * (depth_turn.astype(jnp.float32) / depth + step_turn.astype(jnp.float32) / steps)

def forward_plane(depth, steps, depth_modes, step_modes):
    phases = plane_phases(depth, steps, depth_modes, step_modes)
    table = jnp.stack([jnp.cos(phases), -jnp.sin(phases)], axis=-1) / math.sqrt(depth * steps)
    return table.reshape(depth * steps, -1).astype(jnp.bfloat16)

def inverse_plane(depth, steps, depth_modes, step_modes, factor):
    phases = plane_phases(depth, steps, depth_modes, step_modes)
    table = jnp.stack([jnp.cos(phases), -jnp.sin(phases)], axis=-1) * factor
    return table.reshape(depth * steps, -1).T

def complex_apply(form, real_part, imag_part, table_real, table_imag):
    first = partial(jnp.einsum, form, precision=lax.Precision.HIGHEST)
    return (first(real_part, table_real) - first(imag_part, table_imag), first(real_part, table_imag) + first(imag_part, table_real))

def reference(fields, cotangent, mix_weight, spectral_weight):
    highest = lax.Precision.HIGHEST
    total_modes = MX * MY * MZ * MT
    grid = NX * NY * NZ * NT
    plane_modes = MZ * MT
    forward_zt = forward_plane(NZ, NT, MZ, MT).astype(jnp.float32)
    inverse_zt = inverse_plane(NZ, NT, MZ, MT, math.sqrt(2.0 / total_modes))
    forward_y = line_table(NY, MY, -1.0, 1.0 / math.sqrt(NY))
    forward_x = line_table(NX, MX, -1.0, 1.0 / math.sqrt(NX))
    inverse_y = line_table(NY, MY, 1.0, 1.0)
    inverse_x = line_table(NX, MX, 1.0, 1.0)
    weight_real = spectral_weight[:, 0].astype(jnp.float32)
    weight_imag = spectral_weight[:, 1].astype(jnp.float32)
    mixer = mix_weight.astype(jnp.float32)
    mixing = partial(jnp.einsum, precision=highest)

    def spectrum(field):
        partial_zt = jnp.einsum('scxym,mq->sqxcy', field.astype(jnp.float32), forward_zt, precision=highest)
        split = partial_zt.reshape(S_DEV, plane_modes, 2, NX, C, NY)
        real_part, imag_part = complex_apply('skxcy,yj->skxcj', split[:, :, 0], split[:, :, 1], forward_y[0], forward_y[1])
        real_part, imag_part = complex_apply('skxcj,xi->skcij', real_part, imag_part, forward_x[0], forward_x[1])
        return (real_part.reshape(S_DEV, plane_modes, C, MX * MY), imag_part.reshape(S_DEV, plane_modes, C, MX * MY))

    def synthesis(real_part, imag_part):
        real_part = real_part.reshape(S_DEV, plane_modes, C, MX, MY)
        imag_part = imag_part.reshape(S_DEV, plane_modes, C, MX, MY)
        real_part, imag_part = complex_apply('skoij,xi->skxoj', real_part, imag_part, inverse_x[0], inverse_x[1])
        real_part, imag_part = complex_apply('skxoj,yj->skxoy', real_part, imag_part, inverse_y[0], inverse_y[1])
        joined = jnp.stack([real_part, imag_part], axis=2).reshape(S_DEV, 2 * plane_modes, NX, C, NY)
        return jnp.einsum('sqxoy,qm->soxym', joined, inverse_zt, precision=highest)

    def one_group(pair):
        field, upstream = pair
        spec_real, spec_imag = spectrum(field)
        prod_real = mixing('kcom,skcm->skom', weight_real, spec_real) - mixing('kcom,skcm->skom', weight_imag, spec_imag)
        prod_imag = mixing('kcom,skcm->skom', weight_real, spec_imag) + mixing('kcom,skcm->skom', weight_imag, spec_real)
        spectral = synthesis(prod_real, prod_imag)
        local = jnp.einsum('scxym,co->soxym', field.astype(jnp.float32), mixer, precision=highest)
        before = local + spectral
        layer_out = (0.5 * before * (1.0 + jax.scipy.special.erf(before / math.sqrt(2.0)))).astype(jnp.bfloat16)
        slope_factor = 0.5 * (1.0 + jax.scipy.special.erf(before / math.sqrt(2.0))) + before * jnp.exp(-0.5 * before * before) / math.sqrt(2.0 * math.pi)
        slope = (upstream.astype(jnp.float32) * slope_factor).astype(jnp.bfloat16)
        back_real, back_imag = spectrum(slope)
        scale_grad = math.sqrt(2.0 * grid / total_modes)
        grad_real = scale_grad * (mixing('skcm,skom->kcom', spec_real, back_real) + mixing('skcm,skom->kcom', spec_imag, back_imag))
        grad_imag = scale_grad * (mixing('skcm,skom->kcom', spec_real, back_imag) - mixing('skcm,skom->kcom', spec_imag, back_real))
        group = jnp.stack([grad_real, grad_imag], axis=1).astype(jnp.bfloat16)
        adj_real = mixing('kcom,skom->skcm', weight_real, back_real) + mixing('kcom,skom->skcm', weight_imag, back_imag)
        adj_imag = mixing('kcom,skom->skcm', weight_real, back_imag) - mixing('kcom,skom->skcm', weight_imag, back_real)
        returned = synthesis(adj_real, adj_imag)
        local_back = jnp.einsum('soxym,co->scxym', slope.astype(jnp.float32), mixer, precision=highest)
        field_grad = (local_back + returned).astype(jnp.bfloat16)
        return (layer_out, field_grad, group)
    field_groups = fields.reshape(N_DP, S_DEV, C, NX, NY, NZ * NT)
    upstream_groups = cotangent.reshape(N_DP, S_DEV, C, NX, NY, NZ * NT)
    outputs, gradients, groups = lax.map(one_group, (field_groups, upstream_groups))
    layer_out = outputs.reshape(BATCH, C, NX, NY, NZ * NT)
    field_grad = gradients.reshape(BATCH, C, NX, NY, NZ * NT)
    weight_grad = lax.optimization_barrier(jnp.sum(groups.astype(jnp.float32), axis=0)).astype(jnp.bfloat16)
    return (layer_out, field_grad, weight_grad)
```

```python
from functools import partial
import math

import jax
import jax.numpy as jnp
import ml_dtypes
import numpy as np
from jax import lax
from jax.experimental import pallas as pl
from jax.experimental.pallas import tpu as pltpu
from jax.sharding import PartitionSpec as P

NY = 64
NZ = 64
NT = 4
MX = 16
MY = 16
MZ = 16
MT = 2
MODES = MX * MY
PLANE_MODES = MZ * MT
CELLS = NZ * NT
SLOTS = 2
F32 = jnp.float32
BF16 = jnp.bfloat16
MESH = pl.DeviceIdType.MESH


def rounded(table):
    return np.asarray(table, np.float32).astype(ml_dtypes.bfloat16)


def line_phase(length, mode_count):
    turns = np.arange(length)[:, None] * (np.arange(mode_count) - mode_count // 2)[None, :] % length
    return 2.0 * math.pi / length * turns


def plane_phase():
    cells = np.arange(CELLS)
    modes = np.arange(PLANE_MODES)
    depth = (cells // NT)[:, None] * (modes // MT - MZ // 2)[None, :] % NZ
    step = (cells % NT)[:, None] * (modes % MT)[None, :] % NT
    return 2.0 * math.pi * (depth / NZ + step / NT)


def tables(planes, wide_x):
    phase = plane_phase()
    both = np.stack([np.cos(phase), -np.sin(phase)], axis=0)
    both = both.transpose(0, 2, 1).reshape(2 * PLANE_MODES, CELLS)
    to_zt = both / math.sqrt(CELLS)
    from_zt = both * math.sqrt(2.0 / (MODES * PLANE_MODES))
    py = line_phase(NY, MY)
    cy, sy = np.cos(py), np.sin(py)
    turn_y = np.array([[cy, -sy], [sy, cy]])
    eye = np.eye(planes)
    to_y = np.einsum("abyj,xz->axyzbj", turn_y, eye).reshape(2 * planes * NY, planes * 2 * MY)
    to_y = to_y / math.sqrt(NY * wide_x)
    to_y = np.concatenate([to_y] * SLOTS, axis=1)
    back_y = np.array([[cy, sy], [-sy, cy]])
    from_y = np.einsum("abyj,xz->xajbzy", back_y, eye).reshape(planes * 2 * MY, 2 * planes * NY)
    from_y = np.concatenate([from_y] * SLOTS, axis=0)
    px = line_phase(wide_x, MX)
    cx, sx = np.cos(px), np.sin(px)
    turn_x = np.array([[cx, -sx], [sx, cx]])
    to_x = np.einsum("abxi,jk->xajbik", turn_x, np.eye(MY)).reshape(wide_x * 2 * MY, 2 * MODES)
    return tuple(rounded(t) for t in (to_zt, from_zt, to_y, from_y, to_x))


def dot(a, b, ca=1, cb=0):
    return lax.dot_general(a, b, (((ca,), (cb,)), ((), ())), preferred_element_type=F32)


def first_half(shape):
    return lax.broadcasted_iota(jnp.int32, shape, 1) < shape[1] // 2


def plane_forward(read, channels, count, local_modes, to_zt, to_y, lines, lanes, send):
    width = to_y.shape[0] // 2
    q = PLANE_MODES
    step = 4
    for c0 in range(0, channels, step):
        block = read(c0, step)
        part = dot(to_zt[...], block, 1, 1).astype(BF16)
        for d in range(step):
            rows = pl.ds((c0 + d) * q, q)
            lines[rows, :width] = part[:q, d * width : (d + 1) * width]
            lines[rows, width:] = part[q:, d * width : (d + 1) * width]
    lanes[...] = dot(lines[...], to_y[...])
    half = first_half((channels, lanes.shape[1]))
    for s in range(count):
        low = lanes[pl.ds(s * local_modes, channels, stride=q), :]
        if local_modes > 1:
            high = lanes[pl.ds(s * local_modes + 1, channels, stride=q), :]
            low = jnp.where(half, low, high)
        send[s] = low.astype(BF16)


def plane_inverse(got, channels, count, local_modes, from_zt, from_y, lanes, use):
    q = PLANE_MODES
    width = from_y.shape[1] // 2
    half = first_half((channels, lanes.shape[1]))
    for s in range(count):
        block = got[s].astype(F32)
        lanes[pl.ds(s * local_modes, channels, stride=q), :] = jnp.where(half, block, 0.0)
        if local_modes > 1:
            lanes[pl.ds(s * local_modes + 1, channels, stride=q), :] = jnp.where(half, 0.0, block)
    lines = dot(lanes[...].astype(BF16), from_y[...])
    for o in range(channels):
        rows = lines[o * q : (o + 1) * q]
        pair = jnp.concatenate([rows[:, :width], rows[:, width:]], axis=0)
        use(o, dot(pair.T.astype(BF16), from_zt[...]))


def spread_mix(mix, channels, rows):
    n = channels * rows
    r = lax.broadcasted_iota(jnp.int32, (n, channels), 0) // rows
    c = lax.broadcasted_iota(jnp.int32, (n, channels), 1)
    pick = jnp.where(r == c, 1.0, 0.0).astype(BF16)
    grown = dot(dot(pick, mix).astype(BF16), pick, 1, 1)
    a = lax.broadcasted_iota(jnp.int32, (n, n), 0) % rows
    b = lax.broadcasted_iota(jnp.int32, (n, n), 1) % rows
    return jnp.where(a == b, grown, 0.0).astype(BF16)


def mode_stage(adjoint, count, local_modes, got, weight, to_x, send, spec, after_spec, mid, prod):
    channels = got.shape[1]
    lanes = got.shape[2]
    half = first_half((channels, lanes))
    sides = [[] for _ in range(local_modes)]
    for t in range(count // 2):
        even, odd = got[2 * t].astype(F32), got[2 * t + 1].astype(F32)
        sides[0].append(jnp.where(half, even, pltpu.roll(odd, lanes // 2, 1)))
        if local_modes > 1:
            sides[1].append(jnp.where(half, pltpu.roll(even, lanes // 2, 1), odd))
    rows = jnp.concatenate([jnp.concatenate(side, axis=1) for side in sides], axis=0)
    made = dot(rows.astype(BF16), to_x[...])
    spec[...] = made.astype(BF16)
    after_spec()
    mid[...] = made
    for q in range(local_modes):
        base = q * channels
        if adjoint:
            br = mid[base : base + channels, :MODES]
            bi = mid[base : base + channels, MODES:]

            def step(c, carry):
                wr = weight[q, 0, c].astype(F32)
                wi = weight[q, 1, c].astype(F32)
                row = pl.ds(base + c, 1)
                prod[row, :MODES] = jnp.sum(wr * br + wi * bi, axis=0, keepdims=True)
                prod[row, MODES:] = jnp.sum(wr * bi - wi * br, axis=0, keepdims=True)
                return carry

            lax.fori_loop(0, channels, step, 0, unroll=2)
        else:

            def step(c, carry):
                pr, pi = carry
                wr = weight[q, 0, c].astype(F32)
                wi = weight[q, 1, c].astype(F32)
                sr = mid[pl.ds(base + c, 1), :MODES]
                si = mid[pl.ds(base + c, 1), MODES:]
                return pr + (wr * sr - wi * si), pi + (wr * si + wi * sr)

            zero = jnp.zeros((channels, MODES), F32)
            pr, pi = lax.fori_loop(0, channels, step, (zero, zero), unroll=2)
            prod[base : base + channels, :MODES] = pr
            prod[base : base + channels, MODES:] = pi
    out = dot(prod[...].astype(BF16), to_x[...], 1, 1)
    for t in range(count // 2):
        a = out[:channels, t * lanes : (t + 1) * lanes]
        b = out[-channels:, t * lanes : (t + 1) * lanes]
        send[2 * t] = jnp.where(half, a, pltpu.roll(b, lanes // 2, 1)).astype(BF16)
        send[2 * t + 1] = jnp.where(half, pltpu.roll(a, lanes // 2, 1), b).astype(BF16)


GROUP = 16


def partner(me, r, count):
    if count & (count - 1):
        return lax.rem(me + r, count)
    return me ^ r


def set_mixed(source, spread, field):
    channels, width, cells = field.shape
    for g in range(width // GROUP):
        span = slice(g * GROUP, (g + 1) * GROUP)
        block = source[:, span, :].reshape(channels * GROUP, cells)
        field[:, span, :] = dot(spread, block).reshape(channels, GROUP, cells)


def activation(field, cotangent, layer_out, slope):
    channels, width, _ = field.shape
    rows = width
    blocks = width // rows

    def step(n, carry):
        o = n // blocks
        span = pl.ds(pl.multiple_of(n % blocks * rows, rows), rows)
        v = field[o, span, :]
        bell = 0.5 * (1.0 + lax.erf(v * (1.0 / math.sqrt(2.0))))
        layer_out[o, span, :] = (v * bell).astype(BF16)
        factor = bell + v * jnp.exp(-0.5 * v * v) * (1.0 / math.sqrt(2.0 * math.pi))
        slope[o, span, :] = (cotangent[o, span, :].astype(F32) * factor).astype(BF16)
        return carry

    lax.fori_loop(0, channels * blocks, step, 0)


def outer_stage(local_modes, scale, spec, back, out, left, right):
    groups, rows, _ = spec.shape
    channels = rows // local_modes
    left[...] = spec[...].astype(F32)
    right[...] = back[...].astype(F32) * scale
    for q in range(local_modes):
        base = q * channels

        def step(c, carry):
            real, imag = None, None
            for g in range(groups):
                sr = left[g, pl.ds(base + c, 1), :MODES]
                si = left[g, pl.ds(base + c, 1), MODES:]
                br = right[g, base : base + channels, :MODES]
                bi = right[g, base : base + channels, MODES:]
                re = (sr * br + si * bi).astype(BF16).astype(F32)
                im = (sr * bi - si * br).astype(BF16).astype(F32)
                real = re if g == 0 else real + re
                imag = im if g == 0 else imag + im
            out[q, 0, c] = real.astype(BF16)
            out[q, 1, c] = imag.astype(BF16)
            return carry

        lax.fori_loop(0, channels, step, 0)


CHUNKS = 4


def layer_kernel(
    count, groups, local_modes, scale,
    fields_in, upstream_in, mix_in, weight_in, to_zt_in, from_zt_in, to_y_in, from_y_in, to_x_in,
    result, grads, field, last_got, from_zt, from_y,
    mix, to_zt, to_y, fields, upstream, weight, to_x, slope, lines, lanes, mid, prod,
    left, right, sends, gots, specs, backs,
    load_sem, send_sem, recv_sem, dp_send_sem, dp_recv_sem,
):
    channels = fields.shape[0]
    me = lax.axis_index("space")
    group = lax.axis_index("dp")
    part = channels // CHUNKS

    barrier = pltpu.get_barrier_semaphore()
    for r in reversed(range(1, count)):
        pl.semaphore_signal(
            barrier, inc=1, device_id={"space": partner(me, r, count)}, device_id_type=MESH
        )
    for r in range(1, groups):
        pl.semaphore_signal(
            barrier, inc=1, device_id={"dp": lax.rem(group + r, groups)}, device_id_type=MESH
        )

    small = [
        pltpu.make_async_copy(source, target, load_sem.at[CHUNKS + 3 + n])
        for n, (source, target) in enumerate(
            ((to_zt_in, to_zt), (to_y_in, to_y), (mix_in, mix), (from_y_in, from_y),
             (from_zt_in, from_zt))
        )
    ]
    loads = [
        pltpu.make_async_copy(
            fields_in.at[pl.ds(n * part, part)], fields.at[pl.ds(n * part, part)], load_sem.at[n]
        )
        for n in range(CHUNKS)
    ]
    loads += [
        pltpu.make_async_copy(to_x_in, to_x, load_sem.at[CHUNKS]),
        pltpu.make_async_copy(weight_in, weight, load_sem.at[CHUNKS + 1]),
        pltpu.make_async_copy(upstream_in, upstream, load_sem.at[CHUNKS + 2]),
    ]
    for load in small + loads:
        load.start()

    def exchange(n):
        copies = []
        for r in reversed(range(1, count)):
            peer = partner(me, r, count)
            copies.append(
                pltpu.make_async_remote_copy(
                    src_ref=sends.at[n, peer],
                    dst_ref=gots.at[n, me],
                    send_sem=send_sem.at[n, r],
                    recv_sem=recv_sem.at[n, r],
                    device_id={"space": peer},
                    device_id_type=MESH,
                )
            )
            copies[-1].start()
        gots[n, me] = sends[n, me]
        return copies

    def share(n, ref):
        copies = []
        for r in range(1, groups):
            copies.append(
                pltpu.make_async_remote_copy(
                    src_ref=ref.at[group],
                    dst_ref=ref.at[group],
                    send_sem=dp_send_sem.at[n, r],
                    recv_sem=dp_recv_sem.at[n, r],
                    device_id={"dp": lax.rem(group + r, groups)},
                    device_id_type=MESH,
                )
            )
            copies[-1].start()
        return copies

    def finish(copies):
        for copy in copies:
            copy.wait()

    def read_fields(c, n):
        if c % part == 0:
            loads[c // part].wait()
        return fields[c : c + n].reshape(-1, CELLS)

    def read_slope(c, n):
        return slope[c : c + n].reshape(-1, CELLS)

    small[0].wait()
    small[1].wait()
    plane_forward(
        read_fields, channels, count, local_modes, to_zt, to_y, lines, lanes, sends.at[0]
    )
    pl.semaphore_wait(barrier, count + groups - 2)
    moving = exchange(0)
    for load in small[2:]:
        load.wait()
    set_mixed(fields, spread_mix(mix[...].T, channels, GROUP), field)
    loads[CHUNKS].wait()
    loads[CHUNKS + 1].wait()
    finish(moving)

    shared = []
    mode_stage(
        False, count, local_modes, gots.at[0], weight, to_x, sends.at[1],
        specs.at[group], lambda: shared.extend(share(0, specs)), mid, prod,
    )
    moving = exchange(1)
    loads[CHUNKS + 2].wait()
    finish(moving)

    def add(o, value):
        field[o] += value

    plane_inverse(gots.at[1], channels, count, local_modes, from_zt, from_y, lanes, add)
    activation(field, upstream, result, slope)
    plane_forward(
        read_slope, channels, count, local_modes, to_zt, to_y, lines, lanes, sends.at[2]
    )
    moving = exchange(2)
    set_mixed(slope, spread_mix(mix[...], channels, GROUP), field)
    finish(moving)

    mode_stage(
        True, count, local_modes, gots.at[2], weight, to_x, sends.at[3],
        backs.at[group], lambda: shared.extend(share(1, backs)), mid, prod,
    )
    moving = exchange(3)
    finish(shared)
    outer_stage(local_modes, scale, specs, backs, grads, left, right)
    finish(moving)
    last_got[...] = gots[3]


def last_kernel(
    count, local_modes, got, field, result, grads, from_zt, from_y,
    layer_out, field_grad, weight_grad, lanes, grad, sem,
):
    channels = field.shape[0]
    stores = [
        pltpu.make_async_copy(result, layer_out, sem.at[0]),
        pltpu.make_async_copy(grads, weight_grad, sem.at[1]),
    ]
    for store in stores:
        store.start()
    part = channels // CHUNKS

    def ready(o, value):
        grad[o] = (field[o] + value).astype(BF16)
        if (o + 1) % part == 0:
            span = pl.ds(o + 1 - part, part)
            stores.append(
                pltpu.make_async_copy(
                    grad.at[span], field_grad.at[span], sem.at[2 + o // part]
                )
            )
            stores[-1].start()

    plane_inverse(got, channels, count, local_modes, from_zt, from_y, lanes, ready)
    for store in stores:
        store.wait()


def on_device(fields, cotangent, mix_weight, spectral_weight):
    _, channels, planes, rows_y, cells = fields.shape
    count = lax.axis_size("space")
    local_modes = spectral_weight.shape[0]
    wide_x = planes * count
    width = planes * rows_y
    grid = wide_x * NY * CELLS
    to_zt, from_zt, to_y, from_y, to_x = (jnp.asarray(t) for t in tables(planes, wide_x))
    lane_count = to_y.shape[1]
    scale = math.sqrt(2.0 * grid / (MODES * PLANE_MODES))

    field = fields.reshape(channels, width, cells)
    upstream = cotangent.reshape(channels, width, cells)
    groups = lax.axis_size("dp")
    whole = (channels, width, cells)
    rows = local_modes * channels
    anywhere = pl.BlockSpec(memory_space=pl.ANY)
    inside = pl.BlockSpec(memory_space=pltpu.VMEM)
    message = (4, count, channels, lane_count)
    operands = (
        field, upstream, mix_weight, spectral_weight, to_zt, from_zt, to_y, from_y, to_x
    )
    got_shape = (count, channels, lane_count)
    result, grads, mixed, got, kept_zt, kept_y = pl.pallas_call(
        partial(layer_kernel, count, groups, local_modes, scale),
        out_shape=(
            pltpu.VMEM(whole, BF16),
            pltpu.VMEM(spectral_weight.shape, BF16),
            pltpu.VMEM(whole, F32),
            pltpu.VMEM(got_shape, BF16),
            pltpu.VMEM(from_zt.shape, BF16),
            pltpu.VMEM(from_y.shape, BF16),
        ),
        in_specs=[pl.BlockSpec(memory_space=pltpu.HBM)] * 9,
        out_specs=(inside,) * 6,
        scratch_shapes=[
            pltpu.VMEM(mix_weight.shape, BF16),
            pltpu.VMEM(to_zt.shape, BF16),
            pltpu.VMEM(to_y.shape, BF16),
            pltpu.VMEM(whole, BF16),
            pltpu.VMEM(whole, BF16),
            pltpu.VMEM(spectral_weight.shape, BF16),
            pltpu.VMEM(to_x.shape, BF16),
            pltpu.VMEM(whole, BF16),
            pltpu.VMEM((channels * PLANE_MODES, 2 * width), BF16),
            pltpu.VMEM((channels * PLANE_MODES, lane_count), F32),
            pltpu.VMEM((rows, 2 * MODES), F32),
            pltpu.VMEM((rows, 2 * MODES), F32),
            pltpu.VMEM((groups, rows, 2 * MODES), F32),
            pltpu.VMEM((groups, rows, 2 * MODES), F32),
            pltpu.VMEM(message, BF16),
            pltpu.VMEM(message, BF16),
            pltpu.VMEM((groups, rows, 2 * MODES), BF16),
            pltpu.VMEM((groups, rows, 2 * MODES), BF16),
            pltpu.SemaphoreType.DMA((CHUNKS + 8,)),
            pltpu.SemaphoreType.DMA((4, count)),
            pltpu.SemaphoreType.DMA((4, count)),
            pltpu.SemaphoreType.DMA((2, groups)),
            pltpu.SemaphoreType.DMA((2, groups)),
        ],
        compiler_params=pltpu.CompilerParams(
            collective_id=0, has_side_effects=True, vmem_limit_bytes=44 * 2**20
        ),
        name="layer",
    )(*(pltpu.with_memory_space_constraint(x, pltpu.HBM) for x in operands))
    layer_out, field_grad, weight_grad = pl.pallas_call(
        partial(last_kernel, count, local_modes),
        out_shape=(
            jax.ShapeDtypeStruct(whole, BF16),
            jax.ShapeDtypeStruct(whole, BF16),
            jax.ShapeDtypeStruct(spectral_weight.shape, BF16),
        ),
        in_specs=[inside] * 6,
        out_specs=(anywhere, anywhere, anywhere),
        scratch_shapes=[
            pltpu.VMEM((channels * PLANE_MODES, lane_count), F32),
            pltpu.VMEM(whole, BF16),
            pltpu.SemaphoreType.DMA((2 + CHUNKS,)),
        ],
        compiler_params=pltpu.CompilerParams(vmem_limit_bytes=20 * 2**20),
        name="last",
    )(got, mixed, result, grads, kept_zt, kept_y)
    return (layer_out.reshape(fields.shape), field_grad.reshape(fields.shape), weight_grad)


def solution(mesh):
    placed = (
        P("dp", None, "space", None, None),
        P("dp", None, "space", None, None),
        P(),
        P("space", None, None, None, None),
    )
    return jax.shard_map(
        on_device,
        mesh=mesh,
        in_specs=placed,
        out_specs=(
            P("dp", None, "space", None, None),
            P("dp", None, "space", None, None),
            P("space", None, None, None, None),
        ),
        check_vma=False,
    )
```

```python
from functools import partial
import math

import jax
import jax.numpy as jnp
import ml_dtypes
import numpy as np
from jax import lax
from jax.experimental import pallas as pl
from jax.experimental.pallas import tpu as pltpu
from jax.sharding import PartitionSpec as P

NY = 64
NZ = 64
NT = 4
MX = 16
MY = 16
MZ = 16
MT = 2
MODES = MX * MY
PLANE_MODES = MZ * MT
CELLS = NZ * NT
SLOTS = 2
F32 = jnp.float32
BF16 = jnp.bfloat16
MESH = pl.DeviceIdType.MESH


def rounded(table):
    return np.asarray(table, np.float32).astype(ml_dtypes.bfloat16)


def line_phase(length, mode_count):
    turns = np.arange(length)[:, None] * (np.arange(mode_count) - mode_count // 2)[None, :] % length
    return 2.0 * math.pi / length * turns


def plane_phase():
    cells = np.arange(CELLS)
    modes = np.arange(PLANE_MODES)
    depth = (cells // NT)[:, None] * (modes // MT - MZ // 2)[None, :] % NZ
    step = (cells % NT)[:, None] * (modes % MT)[None, :] % NT
    return 2.0 * math.pi * (depth / NZ + step / NT)


def tables(planes, wide_x):
    phase = plane_phase()
    both = np.stack([np.cos(phase), -np.sin(phase)], axis=0)
    both = both.transpose(0, 2, 1).reshape(2 * PLANE_MODES, CELLS)
    to_zt = both / math.sqrt(CELLS)
    from_zt = both * math.sqrt(2.0 / (MODES * PLANE_MODES))
    py = line_phase(NY, MY)
    cy, sy = np.cos(py), np.sin(py)
    turn_y = np.array([[cy, -sy], [sy, cy]])
    eye = np.eye(planes)
    to_y = np.einsum("abyj,xz->axyzbj", turn_y, eye).reshape(2 * planes * NY, planes * 2 * MY)
    to_y = to_y / math.sqrt(NY * wide_x)
    to_y = np.concatenate([to_y] * SLOTS, axis=1)
    back_y = np.array([[cy, sy], [-sy, cy]])
    from_y = np.einsum("abyj,xz->xajbzy", back_y, eye).reshape(planes * 2 * MY, 2 * planes * NY)
    from_y = np.concatenate([from_y] * SLOTS, axis=0)
    px = line_phase(wide_x, MX)
    cx, sx = np.cos(px), np.sin(px)
    turn_x = np.array([[cx, -sx], [sx, cx]])
    to_x = np.einsum("abxi,jk->xajbik", turn_x, np.eye(MY)).reshape(wide_x * 2 * MY, 2 * MODES)
    return tuple(rounded(t) for t in (to_zt, from_zt, to_y, from_y, to_x))


def dot(a, b, ca=1, cb=0):
    return lax.dot_general(a, b, (((ca,), (cb,)), ((), ())), preferred_element_type=F32)


def first_half(shape):
    return lax.broadcasted_iota(jnp.int32, shape, 1) < shape[1] // 2


def plane_forward(read, first, channels, count, local_modes, to_zt, to_y, lines, lanes, send):
    width = to_y.shape[0] // 2
    q = PLANE_MODES
    step = 4
    for c0 in range(0, channels, step):
        block = read(first + c0, step)
        part = dot(to_zt[...], block, 1, 1).astype(BF16)
        for d in range(step):
            rows = pl.ds((c0 + d) * q, q)
            lines[rows, :width] = part[:q, d * width : (d + 1) * width]
            lines[rows, width:] = part[q:, d * width : (d + 1) * width]
    lanes[...] = dot(lines[...], to_y[...])
    half = first_half((channels, lanes.shape[1]))
    for s in range(count):
        low = lanes[pl.ds(s * local_modes, channels, stride=q), :]
        if local_modes > 1:
            high = lanes[pl.ds(s * local_modes + 1, channels, stride=q), :]
            low = jnp.where(half, low, high)
        send[s] = low.astype(BF16)


def plane_inverse(got, channels, count, local_modes, from_zt, from_y, lanes, use):
    q = PLANE_MODES
    width = from_y.shape[1] // 2
    half = first_half((channels, lanes.shape[1]))
    for s in range(count):
        block = got[s].astype(F32)
        lanes[pl.ds(s * local_modes, channels, stride=q), :] = jnp.where(half, block, 0.0)
        if local_modes > 1:
            lanes[pl.ds(s * local_modes + 1, channels, stride=q), :] = jnp.where(half, 0.0, block)
    lines = dot(lanes[...].astype(BF16), from_y[...])
    for o in range(channels):
        rows = lines[o * q : (o + 1) * q]
        pair = jnp.concatenate([rows[:, :width], rows[:, width:]], axis=0)
        use(o, dot(pair.T.astype(BF16), from_zt[...]))


def spread_mix(mix, channels, rows):
    n = channels * rows
    r = lax.broadcasted_iota(jnp.int32, (n, channels), 0) // rows
    c = lax.broadcasted_iota(jnp.int32, (n, channels), 1)
    pick = jnp.where(r == c, 1.0, 0.0).astype(BF16)
    grown = dot(dot(pick, mix).astype(BF16), pick, 1, 1)
    a = lax.broadcasted_iota(jnp.int32, (n, n), 0) % rows
    b = lax.broadcasted_iota(jnp.int32, (n, n), 1) % rows
    return jnp.where(a == b, grown, 0.0).astype(BF16)


def complex_tables(weight, table):
    local_modes, _, channels = weight.shape[:3]

    def step(n, carry):
        q, c = n // channels, n % channels
        wr = weight[q, 0, c].astype(F32)
        wi = weight[q, 1, c].astype(F32)
        table[0, q, c] = wr
        table[1, q, c] = wi - wr
        table[2, q, c] = wi + wr
        return carry

    lax.fori_loop(0, local_modes * channels, step, 0, unroll=2)


def to_modes(got, count, local_modes, to_x):
    channels, lanes = got.shape[1:]
    half = first_half((channels, lanes))
    sides = [[] for _ in range(local_modes)]
    for t in range(count // 2):
        even, odd = got[2 * t].astype(F32), got[2 * t + 1].astype(F32)
        sides[0].append(jnp.where(half, even, pltpu.roll(odd, lanes // 2, 1)))
        if local_modes > 1:
            sides[1].append(jnp.where(half, pltpu.roll(even, lanes // 2, 1), odd))
    rows = jnp.concatenate([jnp.concatenate(side, axis=1) for side in sides], axis=0)
    return dot(rows.astype(BF16), to_x[...])


def from_modes(rows, count, to_x, send):
    channels, lanes = send.shape[1:]
    half = first_half((channels, lanes))
    out = dot(rows.astype(BF16), to_x[...], 1, 1)
    for t in range(count // 2):
        a = out[:channels, t * lanes : (t + 1) * lanes]
        b = out[-channels:, t * lanes : (t + 1) * lanes]
        send[2 * t] = jnp.where(half, a, pltpu.roll(b, lanes // 2, 1)).astype(BF16)
        send[2 * t + 1] = jnp.where(half, pltpu.roll(a, lanes // 2, 1), b).astype(BF16)


def product(table, first, part, local_modes, mid):
    channels = table.shape[2]
    made = []
    for q in range(local_modes):

        def step(c, carry):
            one, two, three = carry
            row = pl.ds(q * channels + c, 1)
            sr = mid[row, :MODES]
            si = mid[row, MODES:]
            a, d, s = (table[k, q, c, first : first + part, :] for k in range(3))
            return one + a * (sr + si), two + d * sr, three + s * si

        zero = jnp.zeros((part, MODES), F32)
        one, two, three = lax.fori_loop(0, channels, step, (zero, zero, zero), unroll=8)
        made.append(jnp.concatenate([one - three, one + two], axis=1))
    return jnp.concatenate(made, axis=0)


def adjoint(table, first, part, local_modes, made, sums, prod, last):
    channels = table.shape[2]
    for q in range(local_modes):
        br = made[q * part : (q + 1) * part, :MODES]
        bi = made[q * part : (q + 1) * part, MODES:]
        both = br + bi

        def step(c, carry):
            a, d, s = (table[k, q, c, first : first + part, :] for k in range(3))
            one = a * both
            total = jnp.concatenate([one + d * bi, one - s * br], axis=1)
            total = jnp.sum(total.reshape(part // 8, 8, 2 * MODES), axis=0)
            if first:
                total += sums[q, c]
            if last:
                prod[pl.ds(q * channels + c, 1), :] = jnp.sum(total, axis=0, keepdims=True)
            else:
                sums[q, c] = total
            return carry

        lax.fori_loop(0, channels, step, 0, unroll=8)


GROUP = 16


def partner(me, r, count):
    if count & (count - 1):
        return lax.rem(me + r, count)
    return me ^ r


def set_mixed(source, spread, field):
    channels, width, cells = field.shape
    for g in range(width // GROUP):
        span = slice(g * GROUP, (g + 1) * GROUP)
        block = source[:, span, :].reshape(channels * GROUP, cells)
        field[:, span, :] = dot(spread, block).reshape(channels, GROUP, cells)


def activation(v, upstream):
    bell = 0.5 + 0.5 * lax.erf(v * (1.0 / math.sqrt(2.0)))
    peak = jnp.exp2(v * v * (-0.5 * math.log2(math.e)) - 0.5 * math.log2(2.0 * math.pi))
    return (v * bell).astype(BF16), (upstream.astype(F32) * (bell + v * peak)).astype(BF16)


def outer_stage(local_modes, scale, spec, back, out, left, right):
    groups, rows, _ = spec.shape
    channels = rows // local_modes
    left[...] = spec[...].astype(F32)
    right[...] = back[...].astype(F32) * scale
    for q in range(local_modes):
        base = q * channels

        def step(c, carry):
            real, imag = None, None
            for g in range(groups):
                sr = left[g, pl.ds(base + c, 1), :MODES]
                si = left[g, pl.ds(base + c, 1), MODES:]
                br = right[g, base : base + channels, :MODES]
                bi = right[g, base : base + channels, MODES:]
                re = (sr * br + si * bi).astype(BF16).astype(F32)
                im = (sr * bi - si * br).astype(BF16).astype(F32)
                real = re if g == 0 else real + re
                imag = im if g == 0 else imag + im
            out[q, 0, c] = real.astype(BF16)
            out[q, 1, c] = imag.astype(BF16)
            return carry

        lax.fori_loop(0, channels, step, 0)


CHUNKS = 4
PARTS = 2


def layer_kernel(
    count, groups, local_modes, scale,
    fields_in, upstream_in, mix_in, weight_in, to_zt_in, from_zt_in, to_y_in, from_y_in, to_x_in,
    result, grads, field, last_got, from_zt, from_y,
    mix, to_zt, to_y, fields, upstream, weight, to_x, slope, lines, lanes, mid, prod,
    left, right, sends, gots, specs, backs, table, sums,
    load_sem, send_sem, recv_sem, dp_send_sem, dp_recv_sem,
):
    channels = fields.shape[0]
    me = lax.axis_index("space")
    group = lax.axis_index("dp")
    load_part = channels // CHUNKS
    part = channels // PARTS

    barrier = pltpu.get_barrier_semaphore()
    for r in reversed(range(1, count)):
        pl.semaphore_signal(
            barrier, inc=1, device_id={"space": partner(me, r, count)}, device_id_type=MESH
        )
    for r in range(1, groups):
        pl.semaphore_signal(
            barrier, inc=1, device_id={"dp": lax.rem(group + r, groups)}, device_id_type=MESH
        )

    small = [
        pltpu.make_async_copy(source, target, load_sem.at[CHUNKS + 3 + n])
        for n, (source, target) in enumerate(
            ((to_zt_in, to_zt), (to_y_in, to_y), (mix_in, mix), (from_y_in, from_y),
             (from_zt_in, from_zt))
        )
    ]
    loads = [
        pltpu.make_async_copy(
            fields_in.at[pl.ds(n * load_part, load_part)],
            fields.at[pl.ds(n * load_part, load_part)],
            load_sem.at[n],
        )
        for n in range(CHUNKS)
    ]
    loads += [
        pltpu.make_async_copy(to_x_in, to_x, load_sem.at[CHUNKS]),
        pltpu.make_async_copy(weight_in, weight, load_sem.at[CHUNKS + 1]),
        pltpu.make_async_copy(upstream_in, upstream, load_sem.at[CHUNKS + 2]),
    ]
    for load in small + loads:
        load.start()

    def exchange(n, k, many):
        parts = pl.ds(k, many)
        for r in reversed(range(1, count)):
            peer = partner(me, r, count)
            pltpu.make_async_remote_copy(
                src_ref=sends.at[n, peer, parts],
                dst_ref=gots.at[n, me, parts],
                send_sem=send_sem.at[n, k],
                recv_sem=recv_sem.at[n, k],
                device_id={"space": peer},
                device_id_type=MESH,
            ).start()
        gots[n, me, parts] = sends[n, me, parts]
        others = pl.ds(0, count - 1)
        return pltpu.make_async_remote_copy(
            src_ref=sends.at[n, others, parts],
            dst_ref=gots.at[n, others, parts],
            send_sem=send_sem.at[n, k],
            recv_sem=recv_sem.at[n, k],
            device_id={"space": partner(me, 1, count)},
            device_id_type=MESH,
        )

    def share(n, ref):
        copies = []
        for r in range(1, groups):
            copies.append(
                pltpu.make_async_remote_copy(
                    src_ref=ref.at[group],
                    dst_ref=ref.at[group],
                    send_sem=dp_send_sem.at[n],
                    recv_sem=dp_recv_sem.at[n],
                    device_id={"dp": lax.rem(group + r, groups)},
                    device_id_type=MESH,
                )
            )
            copies[-1].start()
        others = ref.at[pl.ds(0, groups - 1)]
        return pltpu.make_async_remote_copy(
            src_ref=others,
            dst_ref=others,
            send_sem=dp_send_sem.at[n],
            recv_sem=dp_recv_sem.at[n],
            device_id={"dp": lax.rem(group + 1, groups)},
            device_id_type=MESH,
        )

    def read_fields(c, n):
        if c % load_part == 0:
            loads[c // load_part].wait()
        return fields[c : c + n].reshape(-1, CELLS)

    def read_slope(c, n):
        return slope[c : c + n].reshape(-1, CELLS)

    def rows_of(q, k):
        return slice(q * channels + k * part, q * channels + (k + 1) * part)

    def keep(made, k, wide, narrow):
        for q in range(local_modes):
            block = made[q * part : (q + 1) * part]
            narrow[group, rows_of(q, k)] = block.astype(BF16)
            if wide is not None:
                wide[rows_of(q, k)] = block

    small[0].wait()
    small[1].wait()
    for k in range(PARTS):
        plane_forward(
            read_fields, k * part, part, count, local_modes, to_zt, to_y, lines, lanes,
            sends.at[0, :, k],
        )
    pl.semaphore_wait(barrier, count + groups - 2)
    moving = exchange(0, 0, PARTS)
    for load in small[2:]:
        load.wait()
    loads[CHUNKS + 1].wait()
    complex_tables(weight, table)
    set_mixed(fields, spread_mix(mix[...].T, channels, GROUP), field)
    loads[CHUNKS].wait()
    loads[CHUNKS + 2].wait()
    moving.wait()

    for k in range(PARTS):
        keep(to_modes(gots.at[0, :, k], count, local_modes, to_x), k, mid, specs)
    moving = []
    for k in range(PARTS):
        made = product(table, k * part, part, local_modes, mid)
        from_modes(made, count, to_x, sends.at[1, :, k])
        moving.append(exchange(1, k, 1))
    shared = [share(0, specs)]

    back = []
    for k in range(PARTS):
        moving[k].wait()

        def activate(o, value):
            c = k * part + o
            result[c], slope[c] = activation(field[c] + value, upstream[c])

        plane_inverse(
            gots.at[1, :, k], part, count, local_modes, from_zt, from_y, lanes, activate
        )
        plane_forward(
            read_slope, k * part, part, count, local_modes, to_zt, to_y, lines, lanes,
            sends.at[2, :, k],
        )
        back.append(exchange(2, k, 1))
    set_mixed(slope, spread_mix(mix[...], channels, GROUP), field)

    for k in range(PARTS):
        back[k].wait()
        made = to_modes(gots.at[2, :, k], count, local_modes, to_x)
        keep(made, k, None, backs)
        adjoint(table, k * part, part, local_modes, made, sums, prod, k == PARTS - 1)
    shared.append(share(1, backs))
    moving = []
    for k in range(PARTS):
        rows = jnp.concatenate([prod[rows_of(q, k)] for q in range(local_modes)], axis=0)
        from_modes(rows, count, to_x, sends.at[3, :, k])
        moving.append(exchange(3, k, 1))
    for copies in shared:
        copies.wait()
    outer_stage(local_modes, scale, specs, backs, grads, left, right)
    for copies in moving:
        copies.wait()
    last_got[...] = gots[3]


def last_kernel(
    count, local_modes, got, field, result, grads, from_zt, from_y,
    layer_out, field_grad, weight_grad, lanes, grad, sem,
):
    channels = field.shape[0]
    many = channels // PARTS
    stores = [
        pltpu.make_async_copy(result, layer_out, sem.at[0]),
        pltpu.make_async_copy(grads, weight_grad, sem.at[1]),
    ]
    for store in stores:
        store.start()
    part = channels // CHUNKS

    for k in range(PARTS):

        def ready(o, value):
            c = k * many + o
            grad[c] = (field[c] + value).astype(BF16)
            if (c + 1) % part == 0:
                span = pl.ds(c + 1 - part, part)
                stores.append(
                    pltpu.make_async_copy(
                        grad.at[span], field_grad.at[span], sem.at[2 + c // part]
                    )
                )
                stores[-1].start()

        plane_inverse(
            got.at[:, k], many, count, local_modes, from_zt, from_y, lanes, ready
        )
    for store in stores:
        store.wait()


def on_device(fields, cotangent, mix_weight, spectral_weight):
    _, channels, planes, rows_y, cells = fields.shape
    count = lax.axis_size("space")
    local_modes = spectral_weight.shape[0]
    wide_x = planes * count
    width = planes * rows_y
    grid = wide_x * NY * CELLS
    to_zt, from_zt, to_y, from_y, to_x = (jnp.asarray(t) for t in tables(planes, wide_x))
    lane_count = to_y.shape[1]
    scale = math.sqrt(2.0 * grid / (MODES * PLANE_MODES))

    field = fields.reshape(channels, width, cells)
    upstream = cotangent.reshape(channels, width, cells)
    groups = lax.axis_size("dp")
    whole = (channels, width, cells)
    rows = local_modes * channels
    anywhere = pl.BlockSpec(memory_space=pl.ANY)
    inside = pl.BlockSpec(memory_space=pltpu.VMEM)
    part = channels // PARTS
    message = (4, count, PARTS, part, lane_count)
    operands = (
        field, upstream, mix_weight, spectral_weight, to_zt, from_zt, to_y, from_y, to_x
    )
    got_shape = message[1:]
    result, grads, mixed, got, kept_zt, kept_y = pl.pallas_call(
        partial(layer_kernel, count, groups, local_modes, scale),
        out_shape=(
            pltpu.VMEM(whole, BF16),
            pltpu.VMEM(spectral_weight.shape, BF16),
            pltpu.VMEM(whole, F32),
            pltpu.VMEM(got_shape, BF16),
            pltpu.VMEM(from_zt.shape, BF16),
            pltpu.VMEM(from_y.shape, BF16),
        ),
        in_specs=[pl.BlockSpec(memory_space=pltpu.HBM)] * 9,
        out_specs=(inside,) * 6,
        scratch_shapes=[
            pltpu.VMEM(mix_weight.shape, BF16),
            pltpu.VMEM(to_zt.shape, BF16),
            pltpu.VMEM(to_y.shape, BF16),
            pltpu.VMEM(whole, BF16),
            pltpu.VMEM(whole, BF16),
            pltpu.VMEM(spectral_weight.shape, BF16),
            pltpu.VMEM(to_x.shape, BF16),
            pltpu.VMEM(whole, BF16),
            pltpu.VMEM((part * PLANE_MODES, 2 * width), BF16),
            pltpu.VMEM((part * PLANE_MODES, lane_count), F32),
            pltpu.VMEM((rows, 2 * MODES), F32),
            pltpu.VMEM((rows, 2 * MODES), F32),
            pltpu.VMEM((groups, rows, 2 * MODES), F32),
            pltpu.VMEM((groups, rows, 2 * MODES), F32),
            pltpu.VMEM(message, BF16),
            pltpu.VMEM(message, BF16),
            pltpu.VMEM((groups, rows, 2 * MODES), BF16),
            pltpu.VMEM((groups, rows, 2 * MODES), BF16),
            pltpu.VMEM((3, local_modes, channels, channels, MODES), F32),
            pltpu.VMEM((local_modes, channels, 8, 2 * MODES), F32),
            pltpu.SemaphoreType.DMA((CHUNKS + 8,)),
            pltpu.SemaphoreType.DMA((4, PARTS)),
            pltpu.SemaphoreType.DMA((4, PARTS)),
            pltpu.SemaphoreType.DMA((2,)),
            pltpu.SemaphoreType.DMA((2,)),
        ],
        compiler_params=pltpu.CompilerParams(
            collective_id=0, has_side_effects=True, vmem_limit_bytes=44 * 2**20
        ),
        name="layer",
    )(*(pltpu.with_memory_space_constraint(x, pltpu.HBM) for x in operands))
    layer_out, field_grad, weight_grad = pl.pallas_call(
        partial(last_kernel, count, local_modes),
        out_shape=(
            jax.ShapeDtypeStruct(whole, BF16),
            jax.ShapeDtypeStruct(whole, BF16),
            jax.ShapeDtypeStruct(spectral_weight.shape, BF16),
        ),
        in_specs=[inside] * 6,
        out_specs=(anywhere, anywhere, anywhere),
        scratch_shapes=[
            pltpu.VMEM((part * PLANE_MODES, lane_count), F32),
            pltpu.VMEM(whole, BF16),
            pltpu.SemaphoreType.DMA((2 + CHUNKS,)),
        ],
        compiler_params=pltpu.CompilerParams(vmem_limit_bytes=20 * 2**20),
        name="last",
    )(got, mixed, result, grads, kept_zt, kept_y)
    return (layer_out.reshape(fields.shape), field_grad.reshape(fields.shape), weight_grad)


def solution(mesh):
    placed = (
        P("dp", None, "space", None, None),
        P("dp", None, "space", None, None),
        P(),
        P("space", None, None, None, None),
    )
    return jax.shard_map(
        on_device,
        mesh=mesh,
        in_specs=placed,
        out_specs=(
            P("dp", None, "space", None, None),
            P("dp", None, "space", None, None),
            P("space", None, None, None, None),
        ),
        check_vma=False,
    )
```

```python
from functools import partial
import math

import jax
import jax.numpy as jnp
import ml_dtypes
import numpy as np
from jax import lax
from jax.experimental import pallas as pl
from jax.experimental.pallas import tpu as pltpu
from jax.sharding import PartitionSpec as P

NY = 64
NZ = 64
NT = 4
MX = 16
MY = 16
MZ = 16
MT = 2
MODES = MX * MY
PLANE_MODES = MZ * MT
CELLS = NZ * NT
SLOTS = 2
F32 = jnp.float32
BF16 = jnp.bfloat16
MESH = pl.DeviceIdType.MESH


def rounded(table):
    return np.asarray(table, np.float32).astype(ml_dtypes.bfloat16)


def line_phase(length, mode_count):
    turns = np.arange(length)[:, None] * (np.arange(mode_count) - mode_count // 2)[None, :] % length
    return 2.0 * math.pi / length * turns


def plane_phase():
    cells = np.arange(CELLS)
    modes = np.arange(PLANE_MODES)
    depth = (cells // NT)[:, None] * (modes // MT - MZ // 2)[None, :] % NZ
    step = (cells % NT)[:, None] * (modes % MT)[None, :] % NT
    return 2.0 * math.pi * (depth / NZ + step / NT)


def tables(planes, wide_x):
    phase = plane_phase()
    both = np.stack([np.cos(phase), -np.sin(phase)], axis=0)
    both = both.transpose(0, 2, 1).reshape(2 * PLANE_MODES, CELLS)
    to_zt = both / math.sqrt(CELLS)
    from_zt = both * math.sqrt(2.0 / (MODES * PLANE_MODES))
    py = line_phase(NY, MY)
    cy, sy = np.cos(py), np.sin(py)
    turn_y = np.array([[cy, -sy], [sy, cy]])
    eye = np.eye(planes)
    to_y = np.einsum("abyj,xz->axyzbj", turn_y, eye).reshape(2 * planes * NY, planes * 2 * MY)
    to_y = to_y / math.sqrt(NY * wide_x)
    to_y = np.concatenate([to_y] * SLOTS, axis=1)
    back_y = np.array([[cy, sy], [-sy, cy]])
    from_y = np.einsum("abyj,xz->xajbzy", back_y, eye).reshape(planes * 2 * MY, 2 * planes * NY)
    from_y = np.concatenate([from_y] * SLOTS, axis=0)
    px = line_phase(wide_x, MX)
    cx, sx = np.cos(px), np.sin(px)
    turn_x = np.array([[cx, -sx], [sx, cx]])
    to_x = np.einsum("abxi,jk->xajbik", turn_x, np.eye(MY)).reshape(wide_x * 2 * MY, 2 * MODES)
    return tuple(rounded(t) for t in (to_zt, from_zt, to_y, from_y, to_x, to_x.T))


def dot(a, b, ca=1, cb=0):
    return lax.dot_general(a, b, (((ca,), (cb,)), ((), ())), preferred_element_type=F32)


def first_half(shape):
    return lax.broadcasted_iota(jnp.int32, shape, 1) < shape[1] // 2


STEP = 4


def to_lines(block, row, to_zt, lines):
    width = lines.shape[1] // 2
    q = PLANE_MODES
    part = dot(to_zt[...], block, 1, 1).astype(BF16)
    for d in range(STEP):
        rows = pl.ds((row + d) * q, q)
        lines[rows, :width] = part[:q, d * width : (d + 1) * width]
        lines[rows, width:] = part[q:, d * width : (d + 1) * width]


def to_message(channels, count, local_modes, to_y, lines, send):
    made = dot(lines[...], to_y[...]).reshape(channels, PLANE_MODES, to_y.shape[1])
    made = jnp.swapaxes(made, 0, 1)
    half = first_half(made.shape[1:])
    for s in range(count):
        low = made[s * local_modes]
        if local_modes > 1:
            low = jnp.where(half, low, made[s * local_modes + 1])
        send[s] = low.astype(BF16)


def plane_inverse(got, channels, count, local_modes, from_zt, from_y, lanes, use):
    q = PLANE_MODES
    width = from_y.shape[1] // 2
    half = first_half((channels, lanes.shape[1]))
    for s in range(count):
        block = got[s].astype(F32)
        lanes[pl.ds(s * local_modes, channels, stride=q), :] = jnp.where(half, block, 0.0)
        if local_modes > 1:
            lanes[pl.ds(s * local_modes + 1, channels, stride=q), :] = jnp.where(half, 0.0, block)
    lines = dot(lanes[...].astype(BF16), from_y[...])
    for o in range(channels):
        rows = lines[o * q : (o + 1) * q]
        pair = jnp.concatenate([rows[:, :width], rows[:, width:]], axis=0)
        use(o, dot(pair.T.astype(BF16), from_zt[...]))


def spread_mix(mix, channels, rows):
    n = channels * rows
    r = lax.broadcasted_iota(jnp.int32, (n, channels), 0) // rows
    c = lax.broadcasted_iota(jnp.int32, (n, channels), 1)
    pick = jnp.where(r == c, 1.0, 0.0).astype(BF16)
    grown = dot(dot(pick, mix).astype(BF16), pick, 1, 1)
    a = lax.broadcasted_iota(jnp.int32, (n, n), 0) % rows
    b = lax.broadcasted_iota(jnp.int32, (n, n), 1) % rows
    return jnp.where(a == b, grown, 0.0).astype(BF16)


def complex_tables(weight, table):
    local_modes, _, channels = weight.shape[:3]

    def step(n, carry):
        q, c = n // channels, n % channels
        wr = weight[q, 0, c].astype(F32)
        wi = weight[q, 1, c].astype(F32)
        table[0, q, c] = wr
        table[1, q, c] = wi - wr
        table[2, q, c] = wi + wr
        return carry

    lax.fori_loop(0, local_modes * channels, step, 0, unroll=2)


def to_modes(got, local_modes, to_x):
    count = len(got)
    channels, lanes = got[0].shape
    half = first_half((channels, lanes))
    sides = [[] for _ in range(local_modes)]
    for t in range(count // 2):
        even, odd = got[2 * t].astype(F32), got[2 * t + 1].astype(F32)
        sides[0].append(jnp.where(half, even, pltpu.roll(odd, lanes // 2, 1)))
        if local_modes > 1:
            sides[1].append(jnp.where(half, pltpu.roll(even, lanes // 2, 1), odd))
    rows = jnp.concatenate([jnp.concatenate(side, axis=1) for side in sides], axis=0)
    return dot(rows.astype(BF16), to_x[...])


def from_modes(rows, count, from_x, send):
    shape, lanes = send.shape[1:], send.shape[-1]
    channels = math.prod(shape[:-1])
    half = first_half((channels, lanes))
    out = dot(rows.astype(BF16), from_x[...])
    for t in range(count // 2):
        a = out[:channels, t * lanes : (t + 1) * lanes]
        b = out[-channels:, t * lanes : (t + 1) * lanes]
        even = jnp.where(half, a, pltpu.roll(b, lanes // 2, 1)).astype(BF16)
        odd = jnp.where(half, pltpu.roll(a, lanes // 2, 1), b).astype(BF16)
        send[2 * t] = even.reshape(shape)
        send[2 * t + 1] = odd.reshape(shape)


def product(table, first, part, local_modes, mid):
    channels = table.shape[2]
    made = []
    for q in range(local_modes):

        def step(c, carry):
            one, two, three = carry
            row = pl.ds(q * channels + c, 1)
            sr = mid[row, :MODES]
            si = mid[row, MODES:]
            a, d, s = (table[k, q, c, first : first + part, :] for k in range(3))
            return one + a * (sr + si), two + d * sr, three + s * si

        zero = jnp.zeros((part, MODES), F32)
        one, two, three = lax.fori_loop(0, channels, step, (zero, zero, zero), unroll=8)
        made.append(jnp.concatenate([one - three, one + two], axis=1))
    return jnp.concatenate(made, axis=0)


def fold(blocks):
    low = lax.broadcasted_iota(jnp.int32, blocks[0].shape, 0)
    span = 4
    while span:
        first = (low & span) == 0
        half = len(blocks) // 2
        blocks = [
            jnp.where(first, a, b) + swap(jnp.where(first, b, a), span)
            for a, b in zip(blocks[:half], blocks[half:])
        ]
        span //= 2
    return blocks[0]


def swap(block, span):
    if span == 4:
        return pltpu.roll(block, 4, 0)
    low = lax.broadcasted_iota(jnp.int32, block.shape, 0)
    return jnp.where((low & span) == 0, pltpu.roll(block, 8 - span, 0), pltpu.roll(block, span, 0))


def adjoint(table, first, part, local_modes, made, sums, prod, last):
    channels = table.shape[2]
    for q in range(local_modes):
        br = made[q * part : (q + 1) * part, :MODES]
        bi = made[q * part : (q + 1) * part, MODES:]
        both = br + bi

        def step(c):
            a, d, s = (table[k, q, c, first : first + part, :] for k in range(3))
            one = a * both
            total = jnp.concatenate([one + d * bi, one - s * br], axis=1)
            total = jnp.sum(total.reshape(part // 8, 8, 2 * MODES), axis=0)
            if first:
                total += sums[q, c]
            return total

        def keep(c, carry):
            sums[q, c] = step(c)
            return carry

        def close(n, carry):
            c = pl.multiple_of(n * 8, 8)
            prod[pl.ds(q * channels + c, 8), :] = fold([step(c + d) for d in range(8)])
            return carry

        if last:
            lax.fori_loop(0, channels // 8, close, 0)
        else:
            lax.fori_loop(0, channels, keep, 0, unroll=8)


GROUP = 16


def partner(me, r, count):
    if count & (count - 1):
        return lax.rem(me + r, count)
    return me ^ r


def set_mixed(source, spread, field):
    channels, width, cells = field.shape
    for g in range(width // GROUP):
        span = slice(g * GROUP, (g + 1) * GROUP)
        block = source[:, span, :].reshape(channels * GROUP, cells)
        field[:, span, :] = dot(spread, block).reshape(channels, GROUP, cells)


def activation(v, upstream):
    bell = 0.5 + 0.5 * lax.erf(v * (1.0 / math.sqrt(2.0)))
    peak = jnp.exp2(v * v * (-0.5 * math.log2(math.e)) - 0.5 * math.log2(2.0 * math.pi))
    return (v * bell).astype(BF16), upstream * (bell + v * peak).astype(BF16)


def outer_stage(local_modes, scale, back, first, out, left, right):
    groups, rows, _ = left.shape
    channels = rows // local_modes
    part = back.shape[1] // local_modes
    right[...] = back[...].astype(F32) * scale
    for q in range(local_modes):

        def step(c, carry):
            real, imag = None, None
            for g in range(groups):
                row = pl.ds(q * channels + c, 1)
                sr = left[g, row, :MODES]
                si = left[g, row, MODES:]
                br = right[g, q * part : (q + 1) * part, :MODES]
                bi = right[g, q * part : (q + 1) * part, MODES:]
                re = (sr * br + si * bi).astype(BF16).astype(F32)
                im = (sr * bi - si * br).astype(BF16).astype(F32)
                real = re if g == 0 else real + re
                imag = im if g == 0 else imag + im
            out[q, 0, c, first : first + part, :] = real.astype(BF16)
            out[q, 1, c, first : first + part, :] = imag.astype(BF16)
            return carry

        lax.fori_loop(0, channels, step, 0, unroll=2)


CHUNKS = 4
PARTS = 2


def layer_kernel(
    count, groups, local_modes, scale,
    fields_in, upstream_in, mix_in, weight_in, to_zt_in, from_zt_in, to_y_in, from_y_in, to_x_in,
    from_x_in, result, grads, field, last_got, from_zt, from_y,
    mix, to_zt, to_y, fields, upstream, weight, to_x, from_x, slope, lines, lanes, mid, prod,
    left, right, sends, gots, specs, backs, table, sums,
    load_sem, send_sem, recv_sem, dp_send_sem, dp_recv_sem,
):
    channels = fields.shape[0]
    me = lax.axis_index("space")
    group = lax.axis_index("dp")
    load_part = channels // CHUNKS
    part = channels // PARTS

    barrier = pltpu.get_barrier_semaphore()
    for r in reversed(range(1, count)):
        pl.semaphore_signal(
            barrier, inc=1, device_id={"space": partner(me, r, count)}, device_id_type=MESH
        )
    for r in range(1, groups):
        pl.semaphore_signal(
            barrier, inc=1, device_id={"dp": lax.rem(group + r, groups)}, device_id_type=MESH
        )

    small = [
        pltpu.make_async_copy(source, target, load_sem.at[CHUNKS + 3 + n])
        for n, (source, target) in enumerate(
            ((to_zt_in, to_zt), (to_y_in, to_y), (mix_in, mix), (from_y_in, from_y),
             (from_zt_in, from_zt), (from_x_in, from_x))
        )
    ]
    loads = [
        pltpu.make_async_copy(
            fields_in.at[pl.ds(n * load_part, load_part)],
            fields.at[pl.ds(n * load_part, load_part)],
            load_sem.at[n],
        )
        for n in range(CHUNKS)
    ]
    loads += [
        pltpu.make_async_copy(weight_in, weight, load_sem.at[CHUNKS + 1]),
        pltpu.make_async_copy(to_x_in, to_x, load_sem.at[CHUNKS]),
        pltpu.make_async_copy(upstream_in, upstream, load_sem.at[CHUNKS + 2]),
    ]
    for load in small[:2] + loads[:CHUNKS]:
        load.start()

    def exchange(n, k, many):
        parts = pl.ds(k, many)
        for r in reversed(range(1, count)):
            peer = partner(me, r, count)
            pltpu.make_async_remote_copy(
                src_ref=sends.at[n, peer, parts],
                dst_ref=gots.at[n, me, parts],
                send_sem=send_sem.at[n, k],
                recv_sem=recv_sem.at[n, k],
                device_id={"space": peer},
                device_id_type=MESH,
            ).start()
        gots[n, me, parts] = sends[n, me, parts]
        others = pl.ds(0, count - 1)
        return pltpu.make_async_remote_copy(
            src_ref=sends.at[n, others, parts],
            dst_ref=gots.at[n, others, parts],
            send_sem=send_sem.at[n, k],
            recv_sem=recv_sem.at[n, k],
            device_id={"space": partner(me, 1, count)},
            device_id_type=MESH,
        )

    def share(n, ref):
        for r in range(1, groups):
            pltpu.make_async_remote_copy(
                src_ref=ref.at[group],
                dst_ref=ref.at[group],
                send_sem=dp_send_sem.at[n],
                recv_sem=dp_recv_sem.at[n],
                device_id={"dp": lax.rem(group + r, groups)},
                device_id_type=MESH,
            ).start()
        others = ref.at[pl.ds(0, groups - 1)]
        return pltpu.make_async_remote_copy(
            src_ref=others,
            dst_ref=others,
            send_sem=dp_send_sem.at[n],
            recv_sem=dp_recv_sem.at[n],
            device_id={"dp": lax.rem(group + 1, groups)},
            device_id_type=MESH,
        )

    def read_fields(c, n):
        if c % load_part == 0:
            loads[c // load_part].wait()
            if c // load_part == CHUNKS - 1:
                for load in loads[CHUNKS:] + small[2:]:
                    load.start()
        return fields[c : c + n].reshape(-1, CELLS)

    def rows_of(q, k):
        return slice(q * channels + k * part, q * channels + (k + 1) * part)

    small[0].wait()
    small[1].wait()
    moving = []
    for k in range(PARTS):
        for o in range(0, part, STEP):
            to_lines(read_fields(k * part + o, STEP), o, to_zt, lines)
        to_message(part, count, local_modes, to_y, lines, sends.at[0, :, k])
        if k == 0:
            pl.semaphore_wait(barrier, count + groups - 2)
        moving.append(exchange(0, k, 1))
    small[2].wait()
    loads[CHUNKS].wait()
    complex_tables(weight, table)
    set_mixed(fields, spread_mix(mix[...].T, channels, GROUP), field)
    for load in small[3:] + loads[CHUNKS + 1 :]:
        load.wait()

    for copies in moving:
        copies.wait()
    made = to_modes([gots[0, s].reshape(channels, -1) for s in range(count)], local_modes, to_x)
    mid[...] = made
    specs[group] = made.astype(BF16)
    moving = []
    for k in range(PARTS):
        made = product(table, k * part, part, local_modes, mid)
        from_modes(made, count, from_x, sends.at[1, :, k])
        moving.append(exchange(1, k, 1))
    shared = [share(0, specs)]

    back = []
    for k in range(PARTS):
        moving[k].wait()

        def activate(o, value):
            c = k * part + o
            result[c], slope[c] = activation(field[c] + value, upstream[c])
            if o % STEP == STEP - 1:
                block = slope[c + 1 - STEP : c + 1].reshape(-1, CELLS)
                to_lines(block, o + 1 - STEP, to_zt, lines)

        plane_inverse(
            gots.at[1, :, k], part, count, local_modes, from_zt, from_y, lanes, activate
        )
        to_message(part, count, local_modes, to_y, lines, sends.at[2, :, k])
        back.append(exchange(2, k, 1))
    set_mixed(slope, spread_mix(mix[...], channels, GROUP), field)

    for k in range(PARTS):
        back[k].wait()
        made = to_modes([gots[2, s, k] for s in range(count)], local_modes, to_x)
        backs[k, group] = made.astype(BF16)
        shared.append(share(1 + k, backs.at[k]))
        adjoint(table, k * part, part, local_modes, made, sums, prod, k == PARTS - 1)
    moving = []
    from_modes(prod[...], count, from_x, sends.at[3])
    moving.append(exchange(3, 0, PARTS))
    shared[0].wait()
    left[...] = specs[...].astype(F32)
    for k in range(PARTS):
        shared[1 + k].wait()
        outer_stage(local_modes, scale, backs.at[k], k * part, grads, left, right)
    for copies in moving:
        copies.wait()
    last_got[...] = gots[3]


def last_kernel(
    count, local_modes, got, field, result, grads, from_zt, from_y,
    layer_out, field_grad, weight_grad, lanes, grad, sem,
):
    channels = field.shape[0]
    many = channels // PARTS
    stores = [
        pltpu.make_async_copy(result, layer_out, sem.at[0]),
        pltpu.make_async_copy(grads, weight_grad, sem.at[1]),
    ]
    for store in stores:
        store.start()
    part = channels // CHUNKS

    for k in range(PARTS):

        def ready(o, value):
            c = k * many + o
            grad[c] = (field[c] + value).astype(BF16)
            if (c + 1) % part == 0:
                span = pl.ds(c + 1 - part, part)
                stores.append(
                    pltpu.make_async_copy(
                        grad.at[span], field_grad.at[span], sem.at[2 + c // part]
                    )
                )
                stores[-1].start()

        plane_inverse(
            got.at[:, k], many, count, local_modes, from_zt, from_y, lanes, ready
        )
    for store in stores:
        store.wait()


def on_device(fields, cotangent, mix_weight, spectral_weight):
    _, channels, planes, rows_y, cells = fields.shape
    count = lax.axis_size("space")
    local_modes = spectral_weight.shape[0]
    wide_x = planes * count
    width = planes * rows_y
    grid = wide_x * NY * CELLS
    to_zt, from_zt, to_y, from_y, to_x, from_x = (jnp.asarray(t) for t in tables(planes, wide_x))
    lane_count = to_y.shape[1]
    scale = math.sqrt(2.0 * grid / (MODES * PLANE_MODES))

    field = fields.reshape(channels, width, cells)
    upstream = cotangent.reshape(channels, width, cells)
    groups = lax.axis_size("dp")
    whole = (channels, width, cells)
    rows = local_modes * channels
    anywhere = pl.BlockSpec(memory_space=pl.ANY)
    inside = pl.BlockSpec(memory_space=pltpu.VMEM)
    part = channels // PARTS
    message = (4, count, PARTS, part, lane_count)
    operands = (
        field, upstream, mix_weight, spectral_weight, to_zt, from_zt, to_y, from_y, to_x,
        from_x,
    )
    got_shape = message[1:]
    result, grads, mixed, got, kept_zt, kept_y = pl.pallas_call(
        partial(layer_kernel, count, groups, local_modes, scale),
        out_shape=(
            pltpu.VMEM(whole, BF16),
            pltpu.VMEM(spectral_weight.shape, BF16),
            pltpu.VMEM(whole, F32),
            pltpu.VMEM(got_shape, BF16),
            pltpu.VMEM(from_zt.shape, BF16),
            pltpu.VMEM(from_y.shape, BF16),
        ),
        in_specs=[pl.BlockSpec(memory_space=pltpu.HBM)] * len(operands),
        out_specs=(inside,) * 6,
        scratch_shapes=[
            pltpu.VMEM(mix_weight.shape, BF16),
            pltpu.VMEM(to_zt.shape, BF16),
            pltpu.VMEM(to_y.shape, BF16),
            pltpu.VMEM(whole, BF16),
            pltpu.VMEM(whole, BF16),
            pltpu.VMEM(spectral_weight.shape, BF16),
            pltpu.VMEM(to_x.shape, BF16),
            pltpu.VMEM(from_x.shape, BF16),
            pltpu.VMEM(whole, BF16),
            pltpu.VMEM((part * PLANE_MODES, 2 * width), BF16),
            pltpu.VMEM((part * PLANE_MODES, lane_count), F32),
            pltpu.VMEM((rows, 2 * MODES), F32),
            pltpu.VMEM((rows, 2 * MODES), F32),
            pltpu.VMEM((groups, rows, 2 * MODES), F32),
            pltpu.VMEM((groups, rows // PARTS, 2 * MODES), F32),
            pltpu.VMEM(message, BF16),
            pltpu.VMEM(message, BF16),
            pltpu.VMEM((groups, rows, 2 * MODES), BF16),
            pltpu.VMEM((PARTS, groups, rows // PARTS, 2 * MODES), BF16),
            pltpu.VMEM((3, local_modes, channels, channels, MODES), F32),
            pltpu.VMEM((local_modes, channels, 8, 2 * MODES), F32),
            pltpu.SemaphoreType.DMA((CHUNKS + 9,)),
            pltpu.SemaphoreType.DMA((4, PARTS)),
            pltpu.SemaphoreType.DMA((4, PARTS)),
            pltpu.SemaphoreType.DMA((1 + PARTS,)),
            pltpu.SemaphoreType.DMA((1 + PARTS,)),
        ],
        compiler_params=pltpu.CompilerParams(
            collective_id=0, has_side_effects=True, vmem_limit_bytes=44 * 2**20
        ),
        name="layer",
    )(*(pltpu.with_memory_space_constraint(x, pltpu.HBM) for x in operands))
    layer_out, field_grad, weight_grad = pl.pallas_call(
        partial(last_kernel, count, local_modes),
        out_shape=(
            jax.ShapeDtypeStruct(whole, BF16),
            jax.ShapeDtypeStruct(whole, BF16),
            jax.ShapeDtypeStruct(spectral_weight.shape, BF16),
        ),
        in_specs=[inside] * 6,
        out_specs=(anywhere, anywhere, anywhere),
        scratch_shapes=[
            pltpu.VMEM((part * PLANE_MODES, lane_count), F32),
            pltpu.VMEM(whole, BF16),
            pltpu.SemaphoreType.DMA((2 + CHUNKS,)),
        ],
        compiler_params=pltpu.CompilerParams(vmem_limit_bytes=20 * 2**20),
        name="last",
    )(got, mixed, result, grads, kept_zt, kept_y)
    return (layer_out.reshape(fields.shape), field_grad.reshape(fields.shape), weight_grad)


def solution(mesh):
    placed = (
        P("dp", None, "space", None, None),
        P("dp", None, "space", None, None),
        P(),
        P("space", None, None, None, None),
    )
    return jax.shard_map(
        on_device,
        mesh=mesh,
        in_specs=placed,
        out_specs=(
            P("dp", None, "space", None, None),
            P("dp", None, "space", None, None),
            P("space", None, None, None, None),
        ),
        check_vma=False,
    )
```

```python
from functools import partial
import math

import jax
import jax.numpy as jnp
import ml_dtypes
import numpy as np
from jax import lax
from jax.experimental import pallas as pl
from jax.experimental.pallas import tpu as pltpu
from jax.sharding import PartitionSpec as P

NY = 64
NZ = 64
NT = 4
MX = 16
MY = 16
MZ = 16
MT = 2
MODES = MX * MY
PLANE_MODES = MZ * MT
CELLS = NZ * NT
SLOTS = 2
F32 = jnp.float32
BF16 = jnp.bfloat16
MESH = pl.DeviceIdType.MESH


def rounded(table):
    return np.asarray(table, np.float32).astype(ml_dtypes.bfloat16)


def line_phase(length, mode_count):
    turns = np.arange(length)[:, None] * (np.arange(mode_count) - mode_count // 2)[None, :] % length
    return 2.0 * math.pi / length * turns


def plane_phase():
    cells = np.arange(CELLS)
    modes = np.arange(PLANE_MODES)
    depth = (cells // NT)[:, None] * (modes // MT - MZ // 2)[None, :] % NZ
    step = (cells % NT)[:, None] * (modes % MT)[None, :] % NT
    return 2.0 * math.pi * (depth / NZ + step / NT)


def tables(planes, wide_x):
    phase = plane_phase()
    both = np.stack([np.cos(phase), -np.sin(phase)], axis=0)
    both = both.transpose(0, 2, 1).reshape(2 * PLANE_MODES, CELLS)
    to_zt = both / math.sqrt(CELLS)
    from_zt = both * math.sqrt(2.0 / (MODES * PLANE_MODES))
    py = line_phase(NY, MY)
    cy, sy = np.cos(py), np.sin(py)
    turn_y = np.array([[cy, -sy], [sy, cy]])
    eye = np.eye(planes)
    to_y = np.einsum("abyj,xz->axyzbj", turn_y, eye).reshape(2 * planes * NY, planes * 2 * MY)
    to_y = to_y / math.sqrt(NY * wide_x)
    to_y = np.concatenate([to_y] * SLOTS, axis=1)
    back_y = np.array([[cy, sy], [-sy, cy]])
    from_y = np.einsum("abyj,xz->xajbzy", back_y, eye).reshape(planes * 2 * MY, 2 * planes * NY)
    from_y = np.concatenate([from_y] * SLOTS, axis=0)
    px = line_phase(wide_x, MX)
    cx, sx = np.cos(px), np.sin(px)
    turn_x = np.array([[cx, -sx], [sx, cx]])
    to_x = np.einsum("abxi,jk->xajbik", turn_x, np.eye(MY)).reshape(wide_x * 2 * MY, 2 * MODES)
    return tuple(rounded(t) for t in (to_zt, from_zt, to_y, from_y, to_x, to_x.T))


def dot(a, b, ca=1, cb=0):
    return lax.dot_general(a, b, (((ca,), (cb,)), ((), ())), preferred_element_type=F32)


def first_half(shape):
    return lax.broadcasted_iota(jnp.int32, shape, 1) < shape[1] // 2


STEP = 4


def to_lines(block, row, to_zt, lines):
    width = lines.shape[1] // 2
    q = PLANE_MODES
    part = dot(to_zt[...], block, 1, 1).astype(BF16)
    for d in range(STEP):
        rows = pl.ds((row + d) * q, q)
        lines[rows, :width] = part[:q, d * width : (d + 1) * width]
        lines[rows, width:] = part[q:, d * width : (d + 1) * width]


def to_message(channels, count, local_modes, to_y, lines, send):
    made = dot(lines[...], to_y[...]).reshape(channels, PLANE_MODES, to_y.shape[1])
    made = jnp.swapaxes(made, 0, 1)
    half = first_half(made.shape[1:])
    for s in range(count):
        low = made[s * local_modes]
        if local_modes > 1:
            low = jnp.where(half, low, made[s * local_modes + 1])
        send[s] = low.astype(BF16)


def plane_inverse(got, channels, count, local_modes, from_zt, from_y, lanes, use):
    q = PLANE_MODES
    width = from_y.shape[1] // 2
    half = first_half((channels, lanes.shape[1]))
    for s in range(count):
        block = got[s].astype(F32)
        lanes[pl.ds(s * local_modes, channels, stride=q), :] = jnp.where(half, block, 0.0)
        if local_modes > 1:
            lanes[pl.ds(s * local_modes + 1, channels, stride=q), :] = jnp.where(half, 0.0, block)
    lines = dot(lanes[...].astype(BF16), from_y[...])
    for o in range(channels):
        rows = lines[o * q : (o + 1) * q]
        pair = jnp.concatenate([rows[:, :width], rows[:, width:]], axis=0)
        use(o, dot(pair.T.astype(BF16), from_zt[...]))


def spread_mix(mix, channels, rows):
    n = channels * rows
    r = lax.broadcasted_iota(jnp.int32, (n, channels), 0) // rows
    c = lax.broadcasted_iota(jnp.int32, (n, channels), 1)
    pick = jnp.where(r == c, 1.0, 0.0).astype(BF16)
    grown = dot(dot(pick, mix).astype(BF16), pick, 1, 1)
    a = lax.broadcasted_iota(jnp.int32, (n, n), 0) % rows
    b = lax.broadcasted_iota(jnp.int32, (n, n), 1) % rows
    return jnp.where(a == b, grown, 0.0).astype(BF16)


def complex_tables(weight, table):
    local_modes, _, channels = weight.shape[:3]

    def step(n, carry):
        q, c = n // channels, n % channels
        wr = weight[q, 0, c].astype(F32)
        wi = weight[q, 1, c].astype(F32)
        table[0, q, c] = wr
        table[1, q, c] = wi - wr
        table[2, q, c] = wi + wr
        return carry

    lax.fori_loop(0, local_modes * channels, step, 0, unroll=2)


def to_modes(got, local_modes, to_x):
    count = len(got)
    channels, lanes = got[0].shape
    half = first_half((channels, lanes))
    sides = [[] for _ in range(local_modes)]
    for t in range(count // 2):
        even, odd = got[2 * t].astype(F32), got[2 * t + 1].astype(F32)
        sides[0].append(jnp.where(half, even, pltpu.roll(odd, lanes // 2, 1)))
        if local_modes > 1:
            sides[1].append(jnp.where(half, pltpu.roll(even, lanes // 2, 1), odd))
    rows = jnp.concatenate([jnp.concatenate(side, axis=1) for side in sides], axis=0)
    return dot(rows.astype(BF16), to_x[...])


def from_modes(rows, first, many, from_x, send):
    shape, lanes = send.shape[1:], send.shape[-1]
    channels = math.prod(shape[:-1])
    half = first_half((channels, lanes))
    start = pl.multiple_of(first * (lanes // 2), lanes // 2 * many)
    out = dot(rows.astype(BF16), from_x[:, pl.ds(start, lanes // 2 * many)])
    for t in range(many // 2):
        a = out[:channels, t * lanes : (t + 1) * lanes]
        b = out[-channels:, t * lanes : (t + 1) * lanes]
        even = jnp.where(half, a, pltpu.roll(b, lanes // 2, 1)).astype(BF16)
        odd = jnp.where(half, pltpu.roll(a, lanes // 2, 1), b).astype(BF16)
        send[first + 2 * t] = even.reshape(shape)
        send[first + 2 * t + 1] = odd.reshape(shape)


def product(table, first, part, local_modes, mid):
    channels = table.shape[2]
    made = []
    for q in range(local_modes):

        def step(c, carry):
            one, two, three = carry
            row = pl.ds(q * channels + c, 1)
            sr = mid[row, :MODES]
            si = mid[row, MODES:]
            a, d, s = (table[k, q, c, first : first + part, :] for k in range(3))
            return one + a * (sr + si), two + d * sr, three + s * si

        zero = jnp.zeros((part, MODES), F32)
        one, two, three = lax.fori_loop(0, channels, step, (zero, zero, zero), unroll=8)
        made.append(jnp.concatenate([one - three, one + two], axis=1))
    return jnp.concatenate(made, axis=0)


def fold(blocks):
    low = lax.broadcasted_iota(jnp.int32, blocks[0].shape, 0)
    span = 4
    while span:
        first = (low & span) == 0
        half = len(blocks) // 2
        blocks = [
            jnp.where(first, a, b) + swap(jnp.where(first, b, a), span)
            for a, b in zip(blocks[:half], blocks[half:])
        ]
        span //= 2
    return blocks[0]


def swap(block, span):
    if span == 4:
        return pltpu.roll(block, 4, 0)
    low = lax.broadcasted_iota(jnp.int32, block.shape, 0)
    return jnp.where((low & span) == 0, pltpu.roll(block, 8 - span, 0), pltpu.roll(block, span, 0))


def adjoint(table, first, part, local_modes, made, sums, prod, last):
    channels = table.shape[2]
    for q in range(local_modes):
        br = made[q * part : (q + 1) * part, :MODES]
        bi = made[q * part : (q + 1) * part, MODES:]
        both = br + bi

        def step(c):
            a, d, s = (table[k, q, c, first : first + part, :] for k in range(3))
            one = a * both
            total = jnp.concatenate([one + d * bi, one - s * br], axis=1)
            total = jnp.sum(total.reshape(part // 8, 8, 2 * MODES), axis=0)
            if first:
                total += sums[q, c]
            return total

        def keep(c, carry):
            sums[q, c] = step(c)
            return carry

        def close(n, carry):
            c = pl.multiple_of(n * 8, 8)
            prod[pl.ds(q * channels + c, 8), :] = fold([step(c + d) for d in range(8)])
            return carry

        if last:
            lax.fori_loop(0, channels // 8, close, 0)
        else:
            lax.fori_loop(0, channels, keep, 0, unroll=8)


GROUP = 16


def partner(me, r, count):
    if count & (count - 1):
        return lax.rem(me + r, count)
    return me ^ r


def set_mixed(source, spread, field):
    channels, width, cells = field.shape
    for g in range(width // GROUP):
        span = slice(g * GROUP, (g + 1) * GROUP)
        block = source[:, span, :].reshape(channels * GROUP, cells)
        field[:, span, :] = dot(spread, block).reshape(channels, GROUP, cells)


def activation(v, upstream):
    bell = 0.5 + 0.5 * lax.erf(v * (1.0 / math.sqrt(2.0)))
    peak = jnp.exp2(v * v * (-0.5 * math.log2(math.e)) - 0.5 * math.log2(2.0 * math.pi))
    return (v * bell).astype(BF16), upstream * (bell + v * peak).astype(BF16)


def outer_stage(local_modes, scale, back, first, out, left, right):
    groups, rows, _ = left.shape
    channels = rows // local_modes
    part = back.shape[1] // local_modes
    right[...] = back[...].astype(F32) * scale
    for q in range(local_modes):

        def step(c, carry):
            real, imag = None, None
            for g in range(groups):
                row = pl.ds(q * channels + c, 1)
                sr = left[g, row, :MODES]
                si = left[g, row, MODES:]
                br = right[g, q * part : (q + 1) * part, :MODES]
                bi = right[g, q * part : (q + 1) * part, MODES:]
                re = (sr * br + si * bi).astype(BF16).astype(F32)
                im = (sr * bi - si * br).astype(BF16).astype(F32)
                real = re if g == 0 else real + re
                imag = im if g == 0 else imag + im
            out[q, 0, c, first : first + part, :] = real.astype(BF16)
            out[q, 1, c, first : first + part, :] = imag.astype(BF16)
            return carry

        lax.fori_loop(0, channels, step, 0, unroll=2)


CHUNKS = 4
PARTS = 2


def layer_kernel(
    count, groups, local_modes, scale,
    fields_in, upstream_in, mix_in, weight_in, to_zt_in, from_zt_in, to_y_in, from_y_in, to_x_in,
    from_x_in, result, grads, field, last_got, from_zt, from_y,
    mix, to_zt, to_y, fields, upstream, weight, to_x, from_x, slope, lines, lanes, mid, prod,
    left, right, sends, gots, specs, backs, table, sums,
    load_sem, send_sem, recv_sem, dp_send_sem, dp_recv_sem,
):
    channels = fields.shape[0]
    me = lax.axis_index("space")
    group = lax.axis_index("dp")
    load_part = channels // CHUNKS
    part = channels // PARTS

    barrier = pltpu.get_barrier_semaphore()
    for r in reversed(range(1, count)):
        pl.semaphore_signal(
            barrier, inc=1, device_id={"space": partner(me, r, count)}, device_id_type=MESH
        )
    for r in range(1, groups):
        pl.semaphore_signal(
            barrier, inc=1, device_id={"dp": lax.rem(group + r, groups)}, device_id_type=MESH
        )

    small = [
        pltpu.make_async_copy(source, target, load_sem.at[CHUNKS + 3 + n])
        for n, (source, target) in enumerate(
            ((to_zt_in, to_zt), (to_y_in, to_y), (mix_in, mix), (from_y_in, from_y),
             (from_zt_in, from_zt), (from_x_in, from_x))
        )
    ]
    loads = [
        pltpu.make_async_copy(
            fields_in.at[pl.ds(n * load_part, load_part)],
            fields.at[pl.ds(n * load_part, load_part)],
            load_sem.at[n],
        )
        for n in range(CHUNKS)
    ]
    loads += [
        pltpu.make_async_copy(weight_in, weight, load_sem.at[CHUNKS + 1]),
        pltpu.make_async_copy(to_x_in, to_x, load_sem.at[CHUNKS]),
        pltpu.make_async_copy(upstream_in, upstream, load_sem.at[CHUNKS + 2]),
    ]
    for load in small[:2] + loads[:CHUNKS]:
        load.start()

    def exchange(n, k, many, order=None):
        parts = pl.ds(k, many)
        for r in order or reversed(range(count)):
            if r == 0:
                gots[n, me, parts] = sends[n, me, parts]
                continue
            peer = partner(me, r, count)
            pltpu.make_async_remote_copy(
                src_ref=sends.at[n, peer, parts],
                dst_ref=gots.at[n, me, parts],
                send_sem=send_sem.at[n, k],
                recv_sem=recv_sem.at[n, k],
                device_id={"space": peer},
                device_id_type=MESH,
            ).start()
        others = pl.ds(0, count - 1)
        return pltpu.make_async_remote_copy(
            src_ref=sends.at[n, others, parts],
            dst_ref=gots.at[n, others, parts],
            send_sem=send_sem.at[n, k],
            recv_sem=recv_sem.at[n, k],
            device_id={"space": partner(me, 1, count)},
            device_id_type=MESH,
        )

    near = 4 if count % 8 == 0 and not count & (count - 1) else count

    def synthesize(rows, n, k, many):
        blocks = count // near
        for g in reversed(range(blocks)):
            first = partner(me // near, g, blocks) * near if g else me // near * near
            if many == 1:
                from_modes(rows, first, near, from_x, sends.at[n, :, k])
            else:
                from_modes(rows, first, near, from_x, sends.at[n])
            arrival = exchange(n, k, many, range(near * g, near * (g + 1))[::-1])
        return arrival

    def share(n, ref):
        for r in range(1, groups):
            pltpu.make_async_remote_copy(
                src_ref=ref.at[group],
                dst_ref=ref.at[group],
                send_sem=dp_send_sem.at[n],
                recv_sem=dp_recv_sem.at[n],
                device_id={"dp": lax.rem(group + r, groups)},
                device_id_type=MESH,
            ).start()
        others = ref.at[pl.ds(0, groups - 1)]
        return pltpu.make_async_remote_copy(
            src_ref=others,
            dst_ref=others,
            send_sem=dp_send_sem.at[n],
            recv_sem=dp_recv_sem.at[n],
            device_id={"dp": lax.rem(group + 1, groups)},
            device_id_type=MESH,
        )

    def read_fields(c, n):
        if c % load_part == 0:
            loads[c // load_part].wait()
            if c // load_part == CHUNKS - 1:
                for load in loads[CHUNKS:] + small[2:]:
                    load.start()
        return fields[c : c + n].reshape(-1, CELLS)

    def rows_of(q, k):
        return slice(q * channels + k * part, q * channels + (k + 1) * part)

    small[0].wait()
    small[1].wait()
    moving = []
    for k in range(PARTS):
        for o in range(0, part, STEP):
            to_lines(read_fields(k * part + o, STEP), o, to_zt, lines)
        to_message(part, count, local_modes, to_y, lines, sends.at[0, :, k])
        if k == 0:
            pl.semaphore_wait(barrier, count + groups - 2)
        moving.append(exchange(0, k, 1))
    small[2].wait()
    loads[CHUNKS].wait()
    complex_tables(weight, table)
    set_mixed(fields, spread_mix(mix[...].T, channels, GROUP), field)
    for load in small[3:] + loads[CHUNKS + 1 :]:
        load.wait()

    for copies in moving:
        copies.wait()
    made = to_modes([gots[0, s].reshape(channels, -1) for s in range(count)], local_modes, to_x)
    mid[...] = made
    specs[group] = made.astype(BF16)
    moving = []
    for k in range(PARTS):
        made = product(table, k * part, part, local_modes, mid)
        moving.append(synthesize(made, 1, k, 1))
    shared = [share(0, specs)]

    back = []
    for k in range(PARTS):
        moving[k].wait()

        def activate(o, value):
            c = k * part + o
            result[c], slope[c] = activation(field[c] + value, upstream[c])
            if o % STEP == STEP - 1:
                block = slope[c + 1 - STEP : c + 1].reshape(-1, CELLS)
                to_lines(block, o + 1 - STEP, to_zt, lines)

        plane_inverse(
            gots.at[1, :, k], part, count, local_modes, from_zt, from_y, lanes, activate
        )
        to_message(part, count, local_modes, to_y, lines, sends.at[2, :, k])
        back.append(exchange(2, k, 1))
    set_mixed(slope, spread_mix(mix[...], channels, GROUP), field)

    for k in range(PARTS):
        back[k].wait()
        made = to_modes([gots[2, s, k] for s in range(count)], local_modes, to_x)
        backs[k, group] = made.astype(BF16)
        shared.append(share(1 + k, backs.at[k]))
        adjoint(table, k * part, part, local_modes, made, sums, prod, k == PARTS - 1)
    moving = []
    moving.append(synthesize(prod[...], 3, 0, PARTS))
    shared[0].wait()
    left[...] = specs[...].astype(F32)
    for k in range(PARTS):
        shared[1 + k].wait()
        outer_stage(local_modes, scale, backs.at[k], k * part, grads, left, right)
    for copies in moving:
        copies.wait()
    last_got[...] = gots[3]


def last_kernel(
    count, local_modes, got, field, result, grads, from_zt, from_y,
    layer_out, field_grad, weight_grad, lanes, grad, sem,
):
    channels = field.shape[0]
    many = channels // PARTS
    stores = [
        pltpu.make_async_copy(result, layer_out, sem.at[0]),
        pltpu.make_async_copy(grads, weight_grad, sem.at[1]),
    ]
    for store in stores:
        store.start()
    part = channels // CHUNKS

    for k in range(PARTS):

        def ready(o, value):
            c = k * many + o
            grad[c] = (field[c] + value).astype(BF16)
            if (c + 1) % part == 0:
                span = pl.ds(c + 1 - part, part)
                stores.append(
                    pltpu.make_async_copy(
                        grad.at[span], field_grad.at[span], sem.at[2 + c // part]
                    )
                )
                stores[-1].start()

        plane_inverse(
            got.at[:, k], many, count, local_modes, from_zt, from_y, lanes, ready
        )
    for store in stores:
        store.wait()


def on_device(fields, cotangent, mix_weight, spectral_weight):
    _, channels, planes, rows_y, cells = fields.shape
    count = lax.axis_size("space")
    local_modes = spectral_weight.shape[0]
    wide_x = planes * count
    width = planes * rows_y
    grid = wide_x * NY * CELLS
    to_zt, from_zt, to_y, from_y, to_x, from_x = (jnp.asarray(t) for t in tables(planes, wide_x))
    lane_count = to_y.shape[1]
    scale = math.sqrt(2.0 * grid / (MODES * PLANE_MODES))

    field = fields.reshape(channels, width, cells)
    upstream = cotangent.reshape(channels, width, cells)
    groups = lax.axis_size("dp")
    whole = (channels, width, cells)
    rows = local_modes * channels
    anywhere = pl.BlockSpec(memory_space=pl.ANY)
    inside = pl.BlockSpec(memory_space=pltpu.VMEM)
    part = channels // PARTS
    message = (4, count, PARTS, part, lane_count)
    operands = (
        field, upstream, mix_weight, spectral_weight, to_zt, from_zt, to_y, from_y, to_x,
        from_x,
    )
    got_shape = message[1:]
    result, grads, mixed, got, kept_zt, kept_y = pl.pallas_call(
        partial(layer_kernel, count, groups, local_modes, scale),
        out_shape=(
            pltpu.VMEM(whole, BF16),
            pltpu.VMEM(spectral_weight.shape, BF16),
            pltpu.VMEM(whole, F32),
            pltpu.VMEM(got_shape, BF16),
            pltpu.VMEM(from_zt.shape, BF16),
            pltpu.VMEM(from_y.shape, BF16),
        ),
        in_specs=[pl.BlockSpec(memory_space=pltpu.HBM)] * len(operands),
        out_specs=(inside,) * 6,
        scratch_shapes=[
            pltpu.VMEM(mix_weight.shape, BF16),
            pltpu.VMEM(to_zt.shape, BF16),
            pltpu.VMEM(to_y.shape, BF16),
            pltpu.VMEM(whole, BF16),
            pltpu.VMEM(whole, BF16),
            pltpu.VMEM(spectral_weight.shape, BF16),
            pltpu.VMEM(to_x.shape, BF16),
            pltpu.VMEM(from_x.shape, BF16),
            pltpu.VMEM(whole, BF16),
            pltpu.VMEM((part * PLANE_MODES, 2 * width), BF16),
            pltpu.VMEM((part * PLANE_MODES, lane_count), F32),
            pltpu.VMEM((rows, 2 * MODES), F32),
            pltpu.VMEM((rows, 2 * MODES), F32),
            pltpu.VMEM((groups, rows, 2 * MODES), F32),
            pltpu.VMEM((groups, rows // PARTS, 2 * MODES), F32),
            pltpu.VMEM(message, BF16),
            pltpu.VMEM(message, BF16),
            pltpu.VMEM((groups, rows, 2 * MODES), BF16),
            pltpu.VMEM((PARTS, groups, rows // PARTS, 2 * MODES), BF16),
            pltpu.VMEM((3, local_modes, channels, channels, MODES), F32),
            pltpu.VMEM((local_modes, channels, 8, 2 * MODES), F32),
            pltpu.SemaphoreType.DMA((CHUNKS + 9,)),
            pltpu.SemaphoreType.DMA((4, PARTS)),
            pltpu.SemaphoreType.DMA((4, PARTS)),
            pltpu.SemaphoreType.DMA((1 + PARTS,)),
            pltpu.SemaphoreType.DMA((1 + PARTS,)),
        ],
        compiler_params=pltpu.CompilerParams(
            collective_id=0, has_side_effects=True, vmem_limit_bytes=44 * 2**20
        ),
        name="layer",
    )(*(pltpu.with_memory_space_constraint(x, pltpu.HBM) for x in operands))
    layer_out, field_grad, weight_grad = pl.pallas_call(
        partial(last_kernel, count, local_modes),
        out_shape=(
            jax.ShapeDtypeStruct(whole, BF16),
            jax.ShapeDtypeStruct(whole, BF16),
            jax.ShapeDtypeStruct(spectral_weight.shape, BF16),
        ),
        in_specs=[inside] * 6,
        out_specs=(anywhere, anywhere, anywhere),
        scratch_shapes=[
            pltpu.VMEM((part * PLANE_MODES, lane_count), F32),
            pltpu.VMEM(whole, BF16),
            pltpu.SemaphoreType.DMA((2 + CHUNKS,)),
        ],
        compiler_params=pltpu.CompilerParams(vmem_limit_bytes=20 * 2**20),
        name="last",
    )(got, mixed, result, grads, kept_zt, kept_y)
    return (layer_out.reshape(fields.shape), field_grad.reshape(fields.shape), weight_grad)


def solution(mesh):
    placed = (
        P("dp", None, "space", None, None),
        P("dp", None, "space", None, None),
        P(),
        P("space", None, None, None, None),
    )
    return jax.shard_map(
        on_device,
        mesh=mesh,
        in_specs=placed,
        out_specs=(
            P("dp", None, "space", None, None),
            P("dp", None, "space", None, None),
            P("space", None, None, None, None),
        ),
        check_vma=False,
    )
```

```python
from functools import partial
import math

import jax
import jax.numpy as jnp
import ml_dtypes
import numpy as np
from jax import lax
from jax.experimental import pallas as pl
from jax.experimental.pallas import tpu as pltpu
from jax.sharding import PartitionSpec as P

NY = 64
NZ = 64
NT = 4
MX = 16
MY = 16
MZ = 16
MT = 2
MODES = MX * MY
PLANE_MODES = MZ * MT
CELLS = NZ * NT
SLOTS = 2
F32 = jnp.float32
BF16 = jnp.bfloat16
MESH = pl.DeviceIdType.MESH


def rounded(table):
    return np.asarray(table, np.float32).astype(ml_dtypes.bfloat16)


def line_phase(length, mode_count):
    turns = np.arange(length)[:, None] * (np.arange(mode_count) - mode_count // 2)[None, :] % length
    return 2.0 * math.pi / length * turns


def plane_phase():
    cells = np.arange(CELLS)
    modes = np.arange(PLANE_MODES)
    depth = (cells // NT)[:, None] * (modes // MT - MZ // 2)[None, :] % NZ
    step = (cells % NT)[:, None] * (modes % MT)[None, :] % NT
    return 2.0 * math.pi * (depth / NZ + step / NT)


def tables(planes, wide_x):
    phase = plane_phase()
    both = np.stack([np.cos(phase), -np.sin(phase)], axis=0)
    both = both.transpose(0, 2, 1).reshape(2 * PLANE_MODES, CELLS)
    to_zt = both / math.sqrt(CELLS)
    from_zt = both * math.sqrt(2.0 / (MODES * PLANE_MODES))
    py = line_phase(NY, MY)
    cy, sy = np.cos(py), np.sin(py)
    turn_y = np.array([[cy, -sy], [sy, cy]])
    eye = np.eye(planes)
    to_y = np.einsum("abyj,xz->axyzbj", turn_y, eye).reshape(2 * planes * NY, planes * 2 * MY)
    to_y = to_y / math.sqrt(NY * wide_x)
    to_y = np.concatenate([to_y] * SLOTS, axis=1)
    back_y = np.array([[cy, sy], [-sy, cy]])
    from_y = np.einsum("abyj,xz->xajbzy", back_y, eye).reshape(planes * 2 * MY, 2 * planes * NY)
    from_y = np.concatenate([from_y] * SLOTS, axis=0)
    px = line_phase(wide_x, MX)
    cx, sx = np.cos(px), np.sin(px)
    turn_x = np.array([[cx, -sx], [sx, cx]])
    to_x = np.einsum("abxi,jk->xajbik", turn_x, np.eye(MY)).reshape(wide_x * 2 * MY, 2 * MODES)
    return tuple(rounded(t) for t in (to_zt, from_zt, to_y, from_y, to_x, to_x.T))


def dot(a, b, ca=1, cb=0):
    return lax.dot_general(a, b, (((ca,), (cb,)), ((), ())), preferred_element_type=F32)


def first_half(shape):
    return lax.broadcasted_iota(jnp.int32, shape, 1) < shape[1] // 2


STEP = 4


def to_lines(block, row, to_zt, lines):
    width = lines.shape[1] // 2
    q = PLANE_MODES
    part = dot(to_zt[...], block, 1, 1).astype(BF16)
    for d in range(STEP):
        rows = pl.ds((row + d) * q, q)
        lines[rows, :width] = part[:q, d * width : (d + 1) * width]
        lines[rows, width:] = part[q:, d * width : (d + 1) * width]


def to_message(channels, count, local_modes, to_y, lines, send):
    made = dot(lines[...], to_y[...]).reshape(channels, PLANE_MODES, to_y.shape[1])
    made = jnp.swapaxes(made, 0, 1)
    half = first_half(made.shape[1:])
    for s in range(count):
        low = made[s * local_modes]
        if local_modes > 1:
            low = jnp.where(half, low, made[s * local_modes + 1])
        send[s] = low.astype(BF16)


def plane_inverse(got, channels, count, local_modes, from_zt, from_y, lanes, use):
    q = PLANE_MODES
    width = from_y.shape[1] // 2
    half = first_half((channels, lanes.shape[1]))
    for s in range(count):
        block = got[s].astype(F32)
        lanes[pl.ds(s * local_modes, channels, stride=q), :] = jnp.where(half, block, 0.0)
        if local_modes > 1:
            lanes[pl.ds(s * local_modes + 1, channels, stride=q), :] = jnp.where(half, 0.0, block)
    lines = dot(lanes[...].astype(BF16), from_y[...])
    for o in range(channels):
        rows = lines[o * q : (o + 1) * q]
        pair = jnp.concatenate([rows[:, :width], rows[:, width:]], axis=0)
        use(o, dot(pair.T.astype(BF16), from_zt[...]))


def spread_mix(mix, channels, rows):
    n = channels * rows
    r = lax.broadcasted_iota(jnp.int32, (n, channels), 0) // rows
    c = lax.broadcasted_iota(jnp.int32, (n, channels), 1)
    pick = jnp.where(r == c, 1.0, 0.0).astype(BF16)
    grown = dot(dot(pick, mix).astype(BF16), pick, 1, 1)
    a = lax.broadcasted_iota(jnp.int32, (n, n), 0) % rows
    b = lax.broadcasted_iota(jnp.int32, (n, n), 1) % rows
    return jnp.where(a == b, grown, 0.0).astype(BF16)


def complex_tables(weight, table):
    local_modes, _, channels = weight.shape[:3]

    def step(n, carry):
        q, c = n // channels, n % channels
        wr = weight[q, 0, c].astype(F32)
        wi = weight[q, 1, c].astype(F32)
        table[0, q, c] = wr
        table[1, q, c] = wi - wr
        table[2, q, c] = wi + wr
        return carry

    lax.fori_loop(0, local_modes * channels, step, 0, unroll=2)


def to_modes(got, local_modes, to_x):
    count = len(got)
    channels, lanes = got[0].shape
    half = first_half((channels, lanes))
    sides = [[] for _ in range(local_modes)]
    for t in range(count // 2):
        even, odd = got[2 * t].astype(F32), got[2 * t + 1].astype(F32)
        sides[0].append(jnp.where(half, even, pltpu.roll(odd, lanes // 2, 1)))
        if local_modes > 1:
            sides[1].append(jnp.where(half, pltpu.roll(even, lanes // 2, 1), odd))
    rows = jnp.concatenate([jnp.concatenate(side, axis=1) for side in sides], axis=0)
    return dot(rows.astype(BF16), to_x[...])


def from_modes(rows, first, many, from_x, send):
    shape, lanes = send.shape[1:], send.shape[-1]
    channels = math.prod(shape[:-1])
    half = first_half((channels, lanes))
    start = pl.multiple_of(first * (lanes // 2), lanes // 2 * many)
    out = dot(rows.astype(BF16), from_x[:, pl.ds(start, lanes // 2 * many)])
    for t in range(many // 2):
        a = out[:channels, t * lanes : (t + 1) * lanes]
        b = out[-channels:, t * lanes : (t + 1) * lanes]
        even = jnp.where(half, a, pltpu.roll(b, lanes // 2, 1)).astype(BF16)
        odd = jnp.where(half, pltpu.roll(a, lanes // 2, 1), b).astype(BF16)
        send[first + 2 * t] = even.reshape(shape)
        send[first + 2 * t + 1] = odd.reshape(shape)


def product(table, first, part, local_modes, mid):
    channels = table.shape[2]
    made = []
    for q in range(local_modes):

        def step(c, carry):
            one, two, three = carry
            row = pl.ds(q * channels + c, 1)
            sr = mid[row, :MODES]
            si = mid[row, MODES:]
            a, d, s = (table[k, q, c, first : first + part, :] for k in range(3))
            return one + a * (sr + si), two + d * sr, three + s * si

        zero = jnp.zeros((part, MODES), F32)
        one, two, three = lax.fori_loop(0, channels, step, (zero, zero, zero), unroll=8)
        made.append(jnp.concatenate([one - three, one + two], axis=1))
    return jnp.concatenate(made, axis=0)


def fold(blocks):
    low = lax.broadcasted_iota(jnp.int32, blocks[0].shape, 0)
    span = 4
    while span:
        first = (low & span) == 0
        half = len(blocks) // 2
        blocks = [
            jnp.where(first, a, b) + swap(jnp.where(first, b, a), span)
            for a, b in zip(blocks[:half], blocks[half:])
        ]
        span //= 2
    return blocks[0]


def swap(block, span):
    if span == 4:
        return pltpu.roll(block, 4, 0)
    low = lax.broadcasted_iota(jnp.int32, block.shape, 0)
    return jnp.where((low & span) == 0, pltpu.roll(block, 8 - span, 0), pltpu.roll(block, span, 0))


def adjoint(table, first, part, local_modes, made, sums, prod, last):
    channels = table.shape[2]
    for q in range(local_modes):
        br = made[q * part : (q + 1) * part, :MODES]
        bi = made[q * part : (q + 1) * part, MODES:]
        both = br + bi

        def step(c):
            a, d, s = (table[k, q, c, first : first + part, :] for k in range(3))
            one = a * both
            total = jnp.concatenate([one + d * bi, one - s * br], axis=1)
            total = jnp.sum(total.reshape(part // 8, 8, 2 * MODES), axis=0)
            if first:
                total += sums[q, c]
            return total

        def keep(c, carry):
            sums[q, c] = step(c)
            return carry

        def close(n, carry):
            c = pl.multiple_of(n * 8, 8)
            prod[pl.ds(q * channels + c, 8), :] = fold([step(c + d) for d in range(8)])
            return carry

        if last:
            lax.fori_loop(0, channels // 8, close, 0)
        else:
            lax.fori_loop(0, channels, keep, 0, unroll=8)


GROUP = 16


def partner(me, r, count):
    if count & (count - 1):
        return lax.rem(me + r, count)
    return me ^ r


def set_mixed(source, spread, field):
    channels, width, cells = field.shape
    for g in range(width // GROUP):
        span = slice(g * GROUP, (g + 1) * GROUP)
        block = source[:, span, :].reshape(channels * GROUP, cells)
        field[:, span, :] = dot(spread, block).reshape(channels, GROUP, cells)


def activation(v, upstream):
    bell = 0.5 + 0.5 * lax.erf(v * (1.0 / math.sqrt(2.0)))
    peak = jnp.exp2(v * v * (-0.5 * math.log2(math.e)) - 0.5 * math.log2(2.0 * math.pi))
    return (v * bell).astype(BF16), upstream * (bell + v * peak).astype(BF16)


def outer_stage(local_modes, scale, back, first, out, left, right):
    groups, rows, _ = left.shape
    channels = rows // local_modes
    part = back.shape[1] // local_modes
    right[...] = back[...].astype(F32) * scale
    for q in range(local_modes):

        def step(c, carry):
            real, imag = None, None
            for g in range(groups):
                row = pl.ds(q * channels + c, 1)
                sr = left[g, row, :MODES]
                si = left[g, row, MODES:]
                br = right[g, q * part : (q + 1) * part, :MODES]
                bi = right[g, q * part : (q + 1) * part, MODES:]
                re = (sr * br + si * bi).astype(BF16).astype(F32)
                im = (sr * bi - si * br).astype(BF16).astype(F32)
                real = re if g == 0 else real + re
                imag = im if g == 0 else imag + im
            out[q, 0, c, first : first + part, :] = real.astype(BF16)
            out[q, 1, c, first : first + part, :] = imag.astype(BF16)
            return carry

        lax.fori_loop(0, channels, step, 0, unroll=2)


CHUNKS = 4
PARTS = 2


def layer_kernel(
    count, groups, local_modes, scale,
    fields_in, upstream_in, mix_in, weight_in, to_zt_in, from_zt_in, to_y_in, from_y_in, to_x_in,
    from_x_in, result, grads, field, last_got, from_zt, from_y,
    mix, to_zt, to_y, fields, upstream, weight, to_x, from_x, slope, lines, lanes, mid, prod,
    left, right, sends, gots, specs, backs, table, sums,
    load_sem, send_sem, recv_sem, dp_send_sem, dp_recv_sem,
):
    channels = fields.shape[0]
    me = lax.axis_index("space")
    group = lax.axis_index("dp")
    load_part = channels // CHUNKS
    part = channels // PARTS

    barrier = pltpu.get_barrier_semaphore()
    for r in reversed(range(1, count)):
        pl.semaphore_signal(
            barrier, inc=1, device_id={"space": partner(me, r, count)}, device_id_type=MESH
        )
    for r in range(1, groups):
        pl.semaphore_signal(
            barrier, inc=1, device_id={"dp": lax.rem(group + r, groups)}, device_id_type=MESH
        )

    small = [
        pltpu.make_async_copy(source, target, load_sem.at[CHUNKS + 3 + n])
        for n, (source, target) in enumerate(
            ((to_zt_in, to_zt), (to_y_in, to_y), (mix_in, mix), (from_y_in, from_y),
             (from_zt_in, from_zt), (from_x_in, from_x))
        )
    ]
    loads = [
        pltpu.make_async_copy(
            fields_in.at[pl.ds(n * load_part, load_part)],
            fields.at[pl.ds(n * load_part, load_part)],
            load_sem.at[n],
        )
        for n in range(CHUNKS)
    ]
    loads += [
        pltpu.make_async_copy(weight_in, weight, load_sem.at[CHUNKS + 1]),
        pltpu.make_async_copy(to_x_in, to_x, load_sem.at[CHUNKS]),
        pltpu.make_async_copy(upstream_in, upstream, load_sem.at[CHUNKS + 2]),
    ]
    for load in small[:2] + loads[:CHUNKS]:
        load.start()

    def exchange(n, k, many, order=None):
        parts = pl.ds(k, many)
        for r in order or reversed(range(count)):
            if r == 0:
                gots[n, me, parts] = sends[n, me, parts]
                continue
            peer = partner(me, r, count)
            pltpu.make_async_remote_copy(
                src_ref=sends.at[n, peer, parts],
                dst_ref=gots.at[n, me, parts],
                send_sem=send_sem.at[n, k],
                recv_sem=recv_sem.at[n, k],
                device_id={"space": peer},
                device_id_type=MESH,
            ).start()
        others = pl.ds(0, count - 1)
        return pltpu.make_async_remote_copy(
            src_ref=sends.at[n, others, parts],
            dst_ref=gots.at[n, others, parts],
            send_sem=send_sem.at[n, k],
            recv_sem=recv_sem.at[n, k],
            device_id={"space": partner(me, 1, count)},
            device_id_type=MESH,
        )

    near = 4 if count % 8 == 0 and not count & (count - 1) else count

    def synthesize(rows, n, k, many):
        blocks = count // near
        for g in reversed(range(blocks)):
            first = partner(me // near, g, blocks) * near if g else me // near * near
            if many == 1:
                from_modes(rows, first, near, from_x, sends.at[n, :, k])
            else:
                from_modes(rows, first, near, from_x, sends.at[n])
            arrival = exchange(n, k, many, range(near * g, near * (g + 1))[::-1])
        return arrival

    def share(n, ref):
        for r in range(1, groups):
            pltpu.make_async_remote_copy(
                src_ref=ref.at[group],
                dst_ref=ref.at[group],
                send_sem=dp_send_sem.at[n],
                recv_sem=dp_recv_sem.at[n],
                device_id={"dp": lax.rem(group + r, groups)},
                device_id_type=MESH,
            ).start()
        others = ref.at[pl.ds(0, groups - 1)]
        return pltpu.make_async_remote_copy(
            src_ref=others,
            dst_ref=others,
            send_sem=dp_send_sem.at[n],
            recv_sem=dp_recv_sem.at[n],
            device_id={"dp": lax.rem(group + 1, groups)},
            device_id_type=MESH,
        )

    def read_fields(c, n):
        if c % load_part == 0:
            loads[c // load_part].wait()
            if c // load_part == CHUNKS - 1:
                for load in loads[CHUNKS:] + small[2:]:
                    load.start()
        return fields[c : c + n].reshape(-1, CELLS)

    def rows_of(q, k):
        return slice(q * channels + k * part, q * channels + (k + 1) * part)

    small[0].wait()
    small[1].wait()
    moving = []
    for k in range(PARTS):
        for o in range(0, part, STEP):
            to_lines(read_fields(k * part + o, STEP), o, to_zt, lines)
        to_message(part, count, local_modes, to_y, lines, sends.at[0, :, k])
    pl.semaphore_wait(barrier, count + groups - 2)
    moving.append(exchange(0, 0, PARTS))
    small[2].wait()
    loads[CHUNKS].wait()
    complex_tables(weight, table)
    set_mixed(fields, spread_mix(mix[...].T, channels, GROUP), field)
    for load in small[3:] + loads[CHUNKS + 1 :]:
        load.wait()

    for copies in moving:
        copies.wait()
    made = to_modes([gots[0, s].reshape(channels, -1) for s in range(count)], local_modes, to_x)
    mid[...] = made
    specs[group] = made.astype(BF16)
    moving = []
    for k in range(PARTS):
        made = product(table, k * part, part, local_modes, mid)
        moving.append(synthesize(made, 1, k, 1))
    shared = [share(0, specs)]

    back = []
    for k in range(PARTS):
        moving[k].wait()

        def activate(o, value):
            c = k * part + o
            result[c], slope[c] = activation(field[c] + value, upstream[c])
            if o % STEP == STEP - 1:
                block = slope[c + 1 - STEP : c + 1].reshape(-1, CELLS)
                to_lines(block, o + 1 - STEP, to_zt, lines)

        plane_inverse(
            gots.at[1, :, k], part, count, local_modes, from_zt, from_y, lanes, activate
        )
        to_message(part, count, local_modes, to_y, lines, sends.at[2, :, k])
        back.append(exchange(2, k, 1))
    set_mixed(slope, spread_mix(mix[...], channels, GROUP), field)

    for k in range(PARTS):
        back[k].wait()
        made = to_modes([gots[2, s, k] for s in range(count)], local_modes, to_x)
        backs[k, group] = made.astype(BF16)
        shared.append(share(1 + k, backs.at[k]))
        adjoint(table, k * part, part, local_modes, made, sums, prod, k == PARTS - 1)
    moving = []
    moving.append(synthesize(prod[...], 3, 0, PARTS))
    shared[0].wait()
    left[...] = specs[...].astype(F32)
    for k in range(PARTS):
        shared[1 + k].wait()
        outer_stage(local_modes, scale, backs.at[k], k * part, grads, left, right)
    for copies in moving:
        copies.wait()
    last_got[...] = gots[3]


def last_kernel(
    count, local_modes, got, field, result, grads, from_zt, from_y,
    layer_out, field_grad, weight_grad, lanes, grad, sem,
):
    channels = field.shape[0]
    many = channels // PARTS
    stores = [
        pltpu.make_async_copy(result, layer_out, sem.at[0]),
        pltpu.make_async_copy(grads, weight_grad, sem.at[1]),
    ]
    for store in stores:
        store.start()
    part = channels // CHUNKS

    for k in range(PARTS):

        def ready(o, value):
            c = k * many + o
            grad[c] = (field[c] + value).astype(BF16)
            if (c + 1) % part == 0:
                span = pl.ds(c + 1 - part, part)
                stores.append(
                    pltpu.make_async_copy(
                        grad.at[span], field_grad.at[span], sem.at[2 + c // part]
                    )
                )
                stores[-1].start()

        plane_inverse(
            got.at[:, k], many, count, local_modes, from_zt, from_y, lanes, ready
        )
    for store in stores:
        store.wait()


def on_device(fields, cotangent, mix_weight, spectral_weight):
    _, channels, planes, rows_y, cells = fields.shape
    count = lax.axis_size("space")
    local_modes = spectral_weight.shape[0]
    wide_x = planes * count
    width = planes * rows_y
    grid = wide_x * NY * CELLS
    to_zt, from_zt, to_y, from_y, to_x, from_x = (jnp.asarray(t) for t in tables(planes, wide_x))
    lane_count = to_y.shape[1]
    scale = math.sqrt(2.0 * grid / (MODES * PLANE_MODES))

    field = fields.reshape(channels, width, cells)
    upstream = cotangent.reshape(channels, width, cells)
    groups = lax.axis_size("dp")
    whole = (channels, width, cells)
    rows = local_modes * channels
    anywhere = pl.BlockSpec(memory_space=pl.ANY)
    inside = pl.BlockSpec(memory_space=pltpu.VMEM)
    part = channels // PARTS
    message = (4, count, PARTS, part, lane_count)
    operands = (
        field, upstream, mix_weight, spectral_weight, to_zt, from_zt, to_y, from_y, to_x,
        from_x,
    )
    got_shape = message[1:]
    result, grads, mixed, got, kept_zt, kept_y = pl.pallas_call(
        partial(layer_kernel, count, groups, local_modes, scale),
        out_shape=(
            pltpu.VMEM(whole, BF16),
            pltpu.VMEM(spectral_weight.shape, BF16),
            pltpu.VMEM(whole, F32),
            pltpu.VMEM(got_shape, BF16),
            pltpu.VMEM(from_zt.shape, BF16),
            pltpu.VMEM(from_y.shape, BF16),
        ),
        in_specs=[pl.BlockSpec(memory_space=pltpu.HBM)] * len(operands),
        out_specs=(inside,) * 6,
        scratch_shapes=[
            pltpu.VMEM(mix_weight.shape, BF16),
            pltpu.VMEM(to_zt.shape, BF16),
            pltpu.VMEM(to_y.shape, BF16),
            pltpu.VMEM(whole, BF16),
            pltpu.VMEM(whole, BF16),
            pltpu.VMEM(spectral_weight.shape, BF16),
            pltpu.VMEM(to_x.shape, BF16),
            pltpu.VMEM(from_x.shape, BF16),
            pltpu.VMEM(whole, BF16),
            pltpu.VMEM((part * PLANE_MODES, 2 * width), BF16),
            pltpu.VMEM((part * PLANE_MODES, lane_count), F32),
            pltpu.VMEM((rows, 2 * MODES), F32),
            pltpu.VMEM((rows, 2 * MODES), F32),
            pltpu.VMEM((groups, rows, 2 * MODES), F32),
            pltpu.VMEM((groups, rows // PARTS, 2 * MODES), F32),
            pltpu.VMEM(message, BF16),
            pltpu.VMEM(message, BF16),
            pltpu.VMEM((groups, rows, 2 * MODES), BF16),
            pltpu.VMEM((PARTS, groups, rows // PARTS, 2 * MODES), BF16),
            pltpu.VMEM((3, local_modes, channels, channels, MODES), F32),
            pltpu.VMEM((local_modes, channels, 8, 2 * MODES), F32),
            pltpu.SemaphoreType.DMA((CHUNKS + 9,)),
            pltpu.SemaphoreType.DMA((4, PARTS)),
            pltpu.SemaphoreType.DMA((4, PARTS)),
            pltpu.SemaphoreType.DMA((1 + PARTS,)),
            pltpu.SemaphoreType.DMA((1 + PARTS,)),
        ],
        compiler_params=pltpu.CompilerParams(
            collective_id=0, has_side_effects=True, vmem_limit_bytes=44 * 2**20
        ),
        name="layer",
    )(*(pltpu.with_memory_space_constraint(x, pltpu.HBM) for x in operands))
    layer_out, field_grad, weight_grad = pl.pallas_call(
        partial(last_kernel, count, local_modes),
        out_shape=(
            jax.ShapeDtypeStruct(whole, BF16),
            jax.ShapeDtypeStruct(whole, BF16),
            jax.ShapeDtypeStruct(spectral_weight.shape, BF16),
        ),
        in_specs=[inside] * 6,
        out_specs=(anywhere, anywhere, anywhere),
        scratch_shapes=[
            pltpu.VMEM((part * PLANE_MODES, lane_count), F32),
            pltpu.VMEM(whole, BF16),
            pltpu.SemaphoreType.DMA((2 + CHUNKS,)),
        ],
        compiler_params=pltpu.CompilerParams(vmem_limit_bytes=20 * 2**20),
        name="last",
    )(got, mixed, result, grads, kept_zt, kept_y)
    return (layer_out.reshape(fields.shape), field_grad.reshape(fields.shape), weight_grad)


def solution(mesh):
    placed = (
        P("dp", None, "space", None, None),
        P("dp", None, "space", None, None),
        P(),
        P("space", None, None, None, None),
    )
    return jax.shard_map(
        on_device,
        mesh=mesh,
        in_specs=placed,
        out_specs=(
            P("dp", None, "space", None, None),
            P("dp", None, "space", None, None),
            P("space", None, None, None, None),
        ),
        check_vma=False,
    )
```
